32 devices in a mesh: rows: 4 (over y, x), cols: 8 (over z, core).
Axes of the slice: x: 2, y: 2, z: 4, core: 2. Of those that a mesh axis runs over, the one named last changes fastest.
Arguments:
- sensitivity: bfloat16 [4, 32, 512, 512], P('rows', 'cols'), may hold values from -0.25 to 0.25
- tile_rows: int32 [4, 32], P('rows', 'cols'), may hold values from 0 to 127, as said below
- tile_cols: int32 [4, 32], P('rows', 'cols'), may hold values from 0 to 1, as said below
- kept_counts: int32 [4, 32], P('rows', 'cols'), may hold values from 0 to 512, as said below
- misfit: float32 [262144], P('rows'), may hold values from -6 to 6
- data_weight: float32 [262144], P('rows'), may hold values from 0.3 to 3
- depth_weight: float32 [8192], P('cols'), may hold values from 0.25 to 3
- density: float32 [8192], P('cols'), may hold values from -6 to 6
Outputs:
- new_density: float32 [8192], P('cols')
- new_misfit: float32 [262144], P(('rows', 'cols'))
The draws below stay inside these ranges and needn't reach their ends.
Inputs may be any that keep to these rules, and one draw needn't show every extreme that they name: Within the 4 slots of one device the pairs (tile_rows, tile_cols) are distinct. Within the 4 slots of one device the pairs (tile_rows, tile_cols) are distinct. A slot with kept_counts 0 is empty, and empty slots come after all live slots of a device; a live slot keeps 512 // 2 or more coefficients; every device has a live slot, and some device has all 4 slots live.
All inputs are finite; a program needn't handle non-finite values.
Results may differ from the reference program's by a relative error of at most 0.033.
Values may be sent and summed in bfloat16 or wider, within the bound.
A program may use at most 64 MiB of HBM per device.

```python
import math
import jax
import jax.numpy as jnp
from jax import lax

TB = 512
DB = 128
MB = 2
SLOTS = 4
ITERS = 4
NDATA = 262144
NCELL = 8192
N_ROWS = 4
N_COLS = 8


def pattern_all(key):
    base_key = jax.random.fold_in(key, 7001)
    device_total = N_ROWS * N_COLS
    key_order, key_live, key_full, key_kept = jax.random.split(base_key, 4)
    device_keys = jax.random.split(key_order, device_total)

    def single(device_key):
        return jax.random.permutation(device_key, DB * MB)[:SLOTS].astype(jnp.int32)
    positions = jax.vmap(single)(device_keys)
    live_total = jax.random.randint(key_live, (device_total,), 1, max(2, SLOTS // 2) + 1)
    heavy_devices = jax.random.permutation(key_full, device_total)[:max(1, device_total // 32)]
    full_device = jnp.zeros((device_total,), jnp.int32).at[heavy_devices].set(1)
    live_total = jnp.where(full_device > 0, SLOTS, live_total)
    slot_index = jnp.arange(SLOTS, dtype=jnp.int32)[None, :]
    kept_draw = jax.random.randint(key_kept, (device_total, SLOTS), TB // 2, TB + 1)
    kept_draw = jnp.where(slot_index == 0, TB, kept_draw)
    kept_values = jnp.where(slot_index < live_total[:, None], kept_draw, 0).astype(jnp.int32)
    rows_values = (positions // MB).astype(jnp.int32)
    cols_values = (positions % MB).astype(jnp.int32)
    shaped = lambda values: values.reshape(N_ROWS, N_COLS * SLOTS)
    return (shaped(rows_values), shaped(cols_values), shaped(kept_values))


def draw_tile_rows(key, part):
    return pattern_all(key)[0]


def draw_tile_cols(key, part):
    return pattern_all(key)[1]


def draw_kept_counts(key, part):
    return pattern_all(key)[2]


def draw_depth_weight(key, part):
    position = jnp.arange(NCELL, dtype=jnp.float32) / NCELL
    trend = 0.5 * jnp.exp(position * jnp.log(3.0))
    roughness = jnp.exp(jax.random.uniform(key, (NCELL,), jnp.float32, jnp.log(0.5), jnp.log(2.0)))
    return (trend * roughness).astype(jnp.float32)


def level_of(own_key, dims, shards, low, high):
    gain, own = 1.0, jax.random.fold_in(own_key, 6)
    for dim, blocks in shards:
        draws = jnp.exp(jax.random.uniform(jax.random.fold_in(own, dim), (blocks,), jnp.float32, low / len(shards), high / len(shards)))
        gain = gain * jnp.repeat(draws, dims[dim] // blocks).reshape([-1 if axis == dim else 1 for axis in range(len(dims))])
    return gain


def bell_draw(rng, shape, width, bound, cuts=(), held_as=jnp.bfloat16):
    factor_of = level_of(rng, shape, cuts, -0.22, 0.18) if cuts else 1.0
    result = jax.random.normal(rng, shape, jnp.float32) * width * factor_of
    return jnp.minimum(jnp.maximum(result, -bound), bound).astype(held_as)


def setup_inputs(seed: int = 0) -> dict:
    splits = jax.random.split(jax.random.key(seed), 9)
    sensitivity = bell_draw(splits[0], (N_ROWS, N_COLS * SLOTS, TB, TB), TB ** -0.5, 0.25, ((0, 4), (1, 8)))
    tile_rows = draw_tile_rows(jax.random.fold_in(splits[8], 71), 0)
    tile_cols = draw_tile_cols(jax.random.fold_in(splits[8], 71), 0)
    kept_counts = draw_kept_counts(jax.random.fold_in(splits[8], 71), 0)
    misfit = bell_draw(splits[4], (NDATA,), 1.0, 6.0, ((0, 4),), jnp.float32)
    data_weight = jnp.clip(jnp.exp(math.log(3.0) - 2.3025851 * jax.random.uniform(splits[5], (NDATA,), jnp.float32) ** level_of(splits[5], (NDATA,), ((0, 4),), -0.2, 0.2)), 0.3, 3.0)
    depth_weight = draw_depth_weight(jax.random.fold_in(splits[8], 71), 0)
    density = bell_draw(splits[7], (NCELL,), 1.0, 6.0, ((0, 8),), jnp.float32)
    return dict(sensitivity=sensitivity, tile_rows=tile_rows, tile_cols=tile_cols, kept_counts=kept_counts, misfit=misfit, data_weight=data_weight, depth_weight=depth_weight, density=density)


damping = 1.0

def haar_matrix(tile_size):
    rows_index = jnp.arange(tile_size, dtype=jnp.int32)[:, None]
    column_index = jnp.arange(tile_size, dtype=jnp.int32)[None, :]
    levels = jnp.zeros_like(rows_index)
    for bit_shift in range(1, tile_size.bit_length()):
        levels = levels + (rows_index >= 1 << bit_shift).astype(jnp.int32)
    support = jnp.right_shift(tile_size, levels)
    offset = (rows_index - jnp.left_shift(1, levels)) * support
    inside = (column_index >= offset) & (column_index < offset + support)
    polarity = jnp.where(column_index < offset + support // 2, 1.0, -1.0)
    detail = jnp.where(inside, polarity, 0.0) / jnp.sqrt(support.astype(jnp.float32))
    coarse = jnp.full((1, tile_size), 1.0 / math.sqrt(tile_size), jnp.float32)
    return jnp.concatenate([coarse, detail[1:].astype(jnp.float32)], axis=0)

def tile_products(sensitivity, vectors, transpose):
    flattened = sensitivity.reshape(N_ROWS * N_COLS, SLOTS, TB, TB)
    stacked = vectors.reshape(N_ROWS * N_COLS, SLOTS, TB)

    def single(item):
        tile_block, vector = item
        if transpose:
            return jnp.einsum('sab,sa->sb', tile_block.astype(jnp.float32), vector.astype(jnp.float32), precision=lax.Precision.HIGHEST)
        return jnp.einsum('sab,sb->sa', tile_block.astype(jnp.float32), vector.astype(jnp.float32), precision=lax.Precision.HIGHEST)
    return lax.map(single, (flattened, stacked)).reshape(N_ROWS, N_COLS * SLOTS, TB)

def reference(sensitivity, tile_rows, tile_cols, kept_counts, misfit, data_weight, depth_weight, density):
    wavelet = haar_matrix(TB)
    live_mask = jnp.arange(TB, dtype=jnp.int32)[None, None, :] < kept_counts[:, :, None]
    group_of_slot = (jnp.arange(N_COLS * SLOTS, dtype=jnp.int32) // SLOTS).astype(jnp.int32)
    col_global = (group_of_slot[None, :] * MB + tile_cols).astype(jnp.int32)
    row_global = (jnp.arange(N_ROWS, dtype=jnp.int32)[:, None] * DB + tile_rows).astype(jnp.int32)

    def forward(cell_values):
        blocks = cell_values.reshape(N_COLS * MB, TB)
        coeffs = jnp.dot(blocks, wavelet.T, precision=lax.Precision.HIGHEST)
        picked = jnp.where(live_mask, coeffs[col_global], 0.0).astype(jnp.bfloat16)
        products = tile_products(sensitivity, picked, False)
        summed = jax.ops.segment_sum(products.reshape(-1, TB), row_global.reshape(-1), num_segments=N_ROWS * DB)
        return summed.reshape(NDATA)

    def adjoint(weighted):
        picked = weighted.reshape(N_ROWS * DB, TB)[row_global]
        products = jnp.where(live_mask, tile_products(sensitivity, picked, True), 0.0)
        block_sums = jax.ops.segment_sum(products.reshape(-1, TB), col_global.reshape(-1), num_segments=N_COLS * MB)
        return jnp.dot(block_sums, wavelet, precision=lax.Precision.HIGHEST).reshape(NCELL)
    squared = data_weight * data_weight
    rhs = depth_weight * adjoint((squared * misfit).astype(jnp.bfloat16)) - damping * density
    solution = jnp.zeros_like(density)
    residual = rhs
    direction = rhs
    change = jnp.zeros_like(misfit)
    norm_now = jnp.sum(residual * residual)
    for iteration in range(ITERS):
        image_data = forward(depth_weight * direction)
        image_cells = depth_weight * adjoint((squared * image_data).astype(jnp.bfloat16)) + damping * direction
        step_length = norm_now / jnp.sum(direction * image_cells)
        solution = solution + step_length * direction
        residual = residual - step_length * image_cells
        change = change + step_length * image_data
        norm_next = jnp.sum(residual * residual)
        direction = residual + norm_next / norm_now * direction
        norm_now = norm_next
    return (density + depth_weight * solution, misfit - change)
```

```python
import functools
import math

import jax
import jax.numpy as jnp
import numpy as np
from jax import lax
from jax.experimental import pallas as pl
from jax.experimental.pallas import tpu as pltpu
from jax.sharding import PartitionSpec as P

ITERS = 4
DAMPING = 1.0
LANES = 128
F32 = jnp.float32
BF16 = jnp.bfloat16


def haar_signs(size):
    signs = np.zeros((size, size), np.float32)
    scale = np.zeros((1, size), np.float32)
    signs[0] = 1.0
    scale[0, 0] = 1.0 / math.sqrt(size)
    for n in range(1, size):
        level = n.bit_length() - 1
        k = n - (1 << level)
        support = size >> level
        signs[n, k * support : k * support + support // 2] = 1.0
        signs[n, k * support + support // 2 : (k + 1) * support] = -1.0
        scale[0, n] = 1.0 / math.sqrt(support)
    return signs, scale


def split3(x):
    hi = x.astype(BF16)
    rest = x - hi.astype(F32)
    mid = rest.astype(BF16)
    low = (rest - mid.astype(F32)).astype(BF16)
    return hi, mid, low


def nn(a, b):
    return lax.dot_general(a, b, (((1,), (0,)), ((), ())), preferred_element_type=F32)


def nt(a, b):
    return lax.dot_general(a, b, (((1,), (1,)), ((), ())), preferred_element_type=F32)


def select_dot(sel, x):
    hi, mid, low = split3(x)
    return nn(sel, hi) + (nn(sel, mid) + nn(sel, low))


def to_rows(x, width):
    q = width // LANES
    return [
        jnp.concatenate([x[i * q + j : i * q + j + 1, :] for j in range(q)], axis=1)
        for i in range(x.shape[0] // q)
    ]


def to_lanes(rows):
    q = rows[0].shape[1] // LANES
    return jnp.concatenate(
        [row[:, j * LANES : (j + 1) * LANES] for row in rows for j in range(q)], axis=0
    )


def haar_apply(dot, rows, matrix):
    m = len(rows)
    parts = [split3(row) for row in rows]
    lhs = jnp.concatenate([p[t].astype(F32) for t in range(3) for p in parts], axis=0).astype(BF16)
    out = dot(lhs, matrix)
    return [out[i : i + 1] + (out[m + i : m + i + 1] + out[2 * m + i : 2 * m + i + 1]) for i in range(m)]


def total(rows):
    acc = rows[0]
    for row in rows[1:]:
        acc = acc + row
    return jnp.sum(acc, axis=1, keepdims=True)


def kernel(
    n_rows, n_cols, slots,
    rows_s, cols_s, kept_s, scale_ref, depth_ref, density_ref,
    tiles_hbm, signs_hbm, misfit_hbm, weight_hbm,
    density_out, misfit_out,
    tiles, signs, misfit, weight,
    idbuf, colbuf, rowbuf, curvbuf, image_ref, match_ref,
    load_sem, id_send, id_recv, col_send, col_recv, row_send, row_recv, curv_send, curv_recv,
):
    size = tiles.shape[-1]
    q = size // LANES
    blocks = depth_ref.shape[0] * LANES // size
    mrows = slots * q
    n = n_cols * mrows
    me_r = lax.axis_index("rows")
    me_c = lax.axis_index("cols")

    loads = [
        pltpu.make_async_copy(src, dst, load_sem.at[i])
        for i, (src, dst) in enumerate(
            ((weight_hbm, weight), (misfit_hbm, misfit), (tiles_hbm, tiles), (signs_hbm, signs))
        )
    ]
    for load in loads:
        load.start()

    barrier = pltpu.get_barrier_semaphore()
    for off in range(1, n_cols):
        pl.semaphore_signal(
            barrier, inc=1, device_id={"cols": lax.rem(me_c + off, n_cols)},
            device_id_type=pl.DeviceIdType.MESH,
        )
    for off in range(1, n_rows):
        pl.semaphore_signal(
            barrier, inc=1, device_id={"rows": lax.rem(me_r + off, n_rows)},
            device_id_type=pl.DeviceIdType.MESH,
        )

    def send(buf, axis, me, count, send_sem, recv_sem):
        for off in range(1, count):
            pltpu.make_async_remote_copy(
                src_ref=buf.at[me],
                dst_ref=buf.at[me],
                send_sem=send_sem,
                recv_sem=recv_sem,
                device_id={axis: lax.rem(me + off, count)},
                device_id_type=pl.DeviceIdType.MESH,
            ).start()

    def wait_bytes(buf, count, sem):
        view = buf.at[pl.ds(0, count - 1)]
        pltpu.make_async_copy(view, view, sem).wait()

    sub = lax.broadcasted_iota(jnp.int32, (q, LANES), 0)
    loads[0].wait()
    own_weight = jnp.concatenate(
        [weight[pl.ds(rows_s[0, s] * q, q), :] for s in range(slots)], axis=0
    )
    own_squared = own_weight * own_weight
    own_codes = jnp.concatenate([rows_s[0, s] * q + sub for s in range(slots)], axis=0)
    idbuf[me_c, 0:mrows, :] = own_squared
    idbuf[me_c, mrows : 2 * mrows, :] = own_codes.astype(F32)
    loads[1].wait()
    own_misfit = jnp.concatenate(
        [misfit[pl.ds(rows_s[0, s] * q, q), :] for s in range(slots)], axis=0
    )

    lane = lax.broadcasted_iota(jnp.int32, (1, size), 1)
    live = [lane < kept_s[0, s] for s in range(slots)]
    hits = [[cols_s[0, s] == b for b in range(blocks)] for s in range(slots)]
    scale = scale_ref[...]
    depth = to_rows(depth_ref[...], size)
    density = to_rows(density_ref[...], size)

    def adjoint_blocks(field):
        sums = [jnp.zeros((1, size), F32) for _ in range(blocks)]
        for s, row in enumerate(to_rows(field, size)):
            product = nn(row.astype(BF16), tiles[s])
            product = jnp.where(live[s], product, 0.0) * scale
            for b in range(blocks):
                sums[b] = sums[b] + jnp.where(hits[s][b], product, 0.0)
        return sums

    def forward_parts(cells):
        coeffs = haar_apply(nt, [depth[b] * cells[b] for b in range(blocks)], signs[...])
        coeffs = [c * scale for c in coeffs]
        products = []
        for s in range(slots):
            picked = jnp.zeros((1, size), F32)
            for b in range(blocks):
                picked = picked + jnp.where(hits[s][b], coeffs[b], 0.0)
            picked = jnp.where(live[s], picked, 0.0).astype(BF16)
            products.append(nt(picked, tiles[s]))
        return to_lanes(products)

    def put_rows(k, sums):
        for b in range(blocks):
            rowbuf[k, me_r, b : b + 1, :] = sums[b]

    def get_rows(k):
        sums = []
        for b in range(blocks):
            acc = rowbuf[k, 0, b : b + 1, :]
            for r in range(1, n_rows):
                acc = acc + rowbuf[k, r, b : b + 1, :]
            sums.append(acc)
        back = haar_apply(nn, sums, signs[...])
        return [depth[b] * back[b] for b in range(blocks)]

    loads[2].wait()
    put_rows(0, adjoint_blocks((own_squared * own_misfit).astype(BF16).astype(F32)))
    rowbuf[0, me_r, blocks : blocks + 1, :] = jnp.zeros((1, size), F32)
    pl.semaphore_wait(barrier, n_cols + n_rows - 2)
    send(rowbuf.at[0], "rows", me_r, n_rows, row_send.at[0], row_recv.at[0])
    send(idbuf, "cols", me_c, n_cols, id_send.at[0], id_recv.at[0])
    loads[3].wait()

    wait_bytes(rowbuf.at[0], n_rows, row_recv.at[0])
    adj = get_rows(0)
    residual = [adj[b] - DAMPING * density[b] for b in range(blocks)]
    direction = None
    solved = None
    norm_prev = dd = None
    parts_dir = image = change = None
    squared = codes = None

    for k in range(ITERS):
        rr_part = total([residual[b] * residual[b] for b in range(blocks)])
        colbuf[k, me_c, mrows : mrows + 1, :] = jnp.broadcast_to(rr_part, (1, LANES))
        if k:
            rd_part = total([residual[b] * direction[b] for b in range(blocks)])
            colbuf[k, me_c, mrows + 1 : mrows + 2, :] = jnp.broadcast_to(rd_part, (1, LANES))
        else:
            colbuf[k, me_c, mrows + 1 : mrows + 2, :] = jnp.zeros((1, LANES), F32)
        colbuf[k, me_c, 0:mrows, :] = forward_parts(residual)
        send(colbuf.at[k], "cols", me_c, n_cols, col_send.at[k], col_recv.at[k])
        if k == 0:
            wait_bytes(idbuf, n_cols, id_recv.at[0])
            codes = idbuf[:, mrows : 2 * mrows, :].reshape(n, LANES)
            squared = idbuf[:, 0:mrows, :].reshape(n, LANES)
            codes_row = jnp.transpose(codes)[0:1, :]
            match_ref[...] = (codes[:, 0:1] == codes_row).astype(F32).astype(BF16)
        wait_bytes(colbuf.at[k], n_cols, col_recv.at[k])
        parts = colbuf[k, :, 0:mrows, :].reshape(n, LANES)
        norm = colbuf[k, 0, mrows : mrows + 1, :]
        cross = colbuf[k, 0, mrows + 1 : mrows + 2, :]
        for c in range(1, n_cols):
            norm = norm + colbuf[k, c, mrows : mrows + 1, :]
            cross = cross + colbuf[k, c, mrows + 1 : mrows + 2, :]
        new_image = select_dot(match_ref[...], parts)
        if k == 0:
            parts_dir, image = parts, new_image
            direction = residual
            dd = norm
        else:
            beta = norm / norm_prev
            beta_row = jnp.concatenate([beta] * q, axis=1)
            parts_dir = parts + beta * parts_dir
            image = new_image + beta * image
            direction = [residual[b] + beta_row * direction[b] for b in range(blocks)]
            dd = norm + 2.0 * beta * cross + beta * beta * dd
        norm_prev = norm
        curv_part = jnp.sum(
            jnp.sum(parts_dir * (squared * image), axis=0, keepdims=True), axis=1, keepdims=True
        )
        if k + 1 < ITERS:
            image_ref[...] = image
            own_image = image_ref[pl.ds(pl.multiple_of(me_c * mrows, mrows), mrows), :]
            put_rows(k + 1, adjoint_blocks(own_squared * own_image))
            rowbuf[k + 1, me_r, blocks : blocks + 1, :] = jnp.broadcast_to(curv_part, (1, size))
            send(rowbuf.at[k + 1], "rows", me_r, n_rows, row_send.at[k + 1], row_recv.at[k + 1])
            wait_bytes(rowbuf.at[k + 1], n_rows, row_recv.at[k + 1])
            curv = rowbuf[k + 1, 0, blocks : blocks + 1, 0:LANES]
            for r in range(1, n_rows):
                curv = curv + rowbuf[k + 1, r, blocks : blocks + 1, 0:LANES]
        else:
            curvbuf[me_r, :, :] = jnp.broadcast_to(curv_part, (8, LANES))
            send(curvbuf, "rows", me_r, n_rows, curv_send.at[0], curv_recv.at[0])
            wait_bytes(curvbuf, n_rows, curv_recv.at[0])
            curv = curvbuf[0, 0:1, :]
            for r in range(1, n_rows):
                curv = curv + curvbuf[r, 0:1, :]
        alpha = norm / (curv + DAMPING * dd)
        alpha_row = jnp.concatenate([alpha] * q, axis=1)
        if k == 0:
            solved = [alpha_row * direction[b] for b in range(blocks)]
            change = alpha * parts_dir
        else:
            solved = [solved[b] + alpha_row * direction[b] for b in range(blocks)]
            change = change + alpha * parts_dir
        if k + 1 < ITERS:
            adj = get_rows(k + 1)
            residual = [
                residual[b] - alpha_row * (adj[b] + DAMPING * direction[b]) for b in range(blocks)
            ]

    density_out[...] = to_lanes([density[b] + depth[b] * solved[b] for b in range(blocks)])
    share = misfit_out.shape[0]
    wanted = (lax.broadcasted_iota(jnp.int32, (share, n), 0) + me_c * share).astype(F32)
    pick = (wanted == jnp.transpose(codes)[0:1, :]).astype(F32).astype(BF16)
    own_share = misfit[pl.ds(pl.multiple_of(me_c * share, 8), share), :]
    misfit_out[...] = own_share - select_dot(pick, change)

    wait_bytes(idbuf, n_cols, id_send.at[0])
    wait_bytes(curvbuf, n_rows, curv_send.at[0])
    for k in range(ITERS):
        wait_bytes(colbuf.at[k], n_cols, col_send.at[k])
        wait_bytes(rowbuf.at[k], n_rows, row_send.at[k])


def per_device(
    n_rows, n_cols,
    sensitivity, tile_rows, tile_cols, kept_counts, misfit, data_weight, depth_weight, density
):
    slots, size = sensitivity.shape[1], sensitivity.shape[-1]
    q = size // LANES
    data_lanes = misfit.shape[0] // LANES
    cell_lanes = density.shape[0] // LANES
    blocks = density.shape[0] // size
    share = data_lanes // n_cols
    mrows = slots * q
    n = n_cols * mrows
    signs, scale = haar_signs(size)
    vmem = pl.BlockSpec(memory_space=pltpu.VMEM)
    smem = pl.BlockSpec(memory_space=pltpu.SMEM)
    anyspace = pl.BlockSpec(memory_space=pl.ANY)
    dma = pltpu.SemaphoreType.DMA
    new_density, new_misfit = pl.pallas_call(
        functools.partial(kernel, n_rows, n_cols, slots),
        out_shape=(
            jax.ShapeDtypeStruct((cell_lanes, LANES), F32),
            jax.ShapeDtypeStruct((share, LANES), F32),
        ),
        in_specs=[smem] * 3 + [vmem] * 3 + [anyspace] * 4,
        out_specs=(vmem, vmem),
        scratch_shapes=[
            pltpu.VMEM((slots, size, size), BF16),
            pltpu.VMEM((size, size), BF16),
            pltpu.VMEM((data_lanes, LANES), F32),
            pltpu.VMEM((data_lanes, LANES), F32),
            pltpu.VMEM((n_cols, 2 * mrows, LANES), F32),
            pltpu.VMEM((ITERS, n_cols, mrows + 8, LANES), F32),
            pltpu.VMEM((ITERS, n_rows, blocks + 2, size), F32),
            pltpu.VMEM((n_rows, 8, LANES), F32),
            pltpu.VMEM((n, LANES), F32),
            pltpu.VMEM((n, n), BF16),
            dma((4,)), dma((1,)), dma((1,)), dma((ITERS,)), dma((ITERS,)),
            dma((ITERS,)), dma((ITERS,)), dma((1,)), dma((1,)),
        ],
        compiler_params=pltpu.CompilerParams(
            collective_id=0, has_side_effects=True, vmem_limit_bytes=48 * 1024 * 1024
        ),
    )(
        tile_rows, tile_cols, kept_counts, jnp.asarray(scale),
        depth_weight.reshape(cell_lanes, LANES), density.reshape(cell_lanes, LANES),
        sensitivity[0], jnp.asarray(signs, BF16),
        misfit.reshape(data_lanes, LANES), data_weight.reshape(data_lanes, LANES),
    )
    return new_density.reshape(-1), new_misfit.reshape(-1)


def solution(mesh):
    return jax.shard_map(
        functools.partial(per_device, mesh.shape["rows"], mesh.shape["cols"]),
        mesh=mesh,
        in_specs=(
            P("rows", "cols", None, None),
            P("rows", "cols"),
            P("rows", "cols"),
            P("rows", "cols"),
            P("rows"),
            P("rows"),
            P("cols"),
            P("cols"),
        ),
        out_specs=(P("cols"), P(("rows", "cols"))),
        check_vma=False,
    )
```

```python
import functools
import math

import jax
import jax.numpy as jnp
import numpy as np
from jax import lax
from jax.experimental import pallas as pl
from jax.experimental.pallas import tpu as pltpu
from jax.sharding import PartitionSpec as P

ITERS = 4
DAMPING = 1.0
LANES = 128
F32 = jnp.float32
BF16 = jnp.bfloat16


def haar_signs(size):
    signs = np.zeros((size, size), np.float32)
    scale = np.zeros((1, size), np.float32)
    signs[0] = 1.0
    scale[0, 0] = 1.0 / math.sqrt(size)
    for n in range(1, size):
        level = n.bit_length() - 1
        k = n - (1 << level)
        support = size >> level
        signs[n, k * support : k * support + support // 2] = 1.0
        signs[n, k * support + support // 2 : (k + 1) * support] = -1.0
        scale[0, n] = 1.0 / math.sqrt(support)
    return signs, scale


def split3(x):
    hi = x.astype(BF16)
    rest = x - hi.astype(F32)
    mid = rest.astype(BF16)
    low = (rest - mid.astype(F32)).astype(BF16)
    return hi, mid, low


def nn(a, b):
    return lax.dot_general(a, b, (((1,), (0,)), ((), ())), preferred_element_type=F32)


def nt(a, b):
    return lax.dot_general(a, b, (((1,), (1,)), ((), ())), preferred_element_type=F32)


def select_dot(sel, x):
    hi, mid, low = split3(x)
    return nn(sel, hi) + (nn(sel, mid) + nn(sel, low))


def to_rows(x, width):
    q = width // LANES
    return [
        jnp.concatenate([x[i * q + j : i * q + j + 1, :] for j in range(q)], axis=1)
        for i in range(x.shape[0] // q)
    ]


def to_lanes(rows):
    q = rows[0].shape[1] // LANES
    return jnp.concatenate(
        [row[:, j * LANES : (j + 1) * LANES] for row in rows for j in range(q)], axis=0
    )


def haar_apply(dot, rows, matrix):
    m = len(rows)
    parts = [split3(row) for row in rows]
    lhs = jnp.concatenate([p[t].astype(F32) for t in range(3) for p in parts], axis=0).astype(BF16)
    out = dot(lhs, matrix)
    return [out[i : i + 1] + (out[m + i : m + i + 1] + out[2 * m + i : 2 * m + i + 1]) for i in range(m)]


def total(rows):
    acc = rows[0]
    for row in rows[1:]:
        acc = acc + row
    return jnp.sum(acc, axis=1, keepdims=True)


def kernel(
    n_rows, n_cols, slots,
    rows_hbm, cols_hbm, kept_hbm, scale_hbm, depth_hbm, density_hbm,
    tiles_hbm, signs_hbm, misfit_hbm, weight_hbm,
    density_out, misfit_out,
    rows_s, cols_s, kept_s, scale_ref, depth_ref, density_ref,
    tiles, signs, misfit, weight,
    idbuf, colbuf, rowbuf, curvbuf, image_ref, match_ref,
    load_sem, id_send, id_recv, col_send, col_recv, row_send, row_recv, curv_send, curv_recv,
):
    size = tiles.shape[-1]
    q = size // LANES
    blocks = depth_ref.shape[0] * LANES // size
    mrows = slots * q
    n = n_cols * mrows
    me_r = lax.axis_index("rows")
    me_c = lax.axis_index("cols")

    loads = [
        pltpu.make_async_copy(src, dst, load_sem.at[i])
        for i, (src, dst) in enumerate(
            (
                (rows_hbm, rows_s), (weight_hbm, weight), (misfit_hbm, misfit),
                (kept_hbm, kept_s), (cols_hbm, cols_s), (scale_hbm, scale_ref),
                (tiles_hbm, tiles), (signs_hbm, signs),
                (depth_hbm, depth_ref), (density_hbm, density_ref),
            )
        )
    ]
    for load in loads:
        load.start()

    barrier = pltpu.get_barrier_semaphore()
    for off in range(1, n_cols):
        pl.semaphore_signal(
            barrier, inc=1, device_id={"cols": lax.rem(me_c + off, n_cols)},
            device_id_type=pl.DeviceIdType.MESH,
        )
    for off in range(1, n_rows):
        pl.semaphore_signal(
            barrier, inc=1, device_id={"rows": lax.rem(me_r + off, n_rows)},
            device_id_type=pl.DeviceIdType.MESH,
        )

    def send(buf, axis, me, count, send_sem, recv_sem):
        for off in range(1, count):
            pltpu.make_async_remote_copy(
                src_ref=buf.at[me],
                dst_ref=buf.at[me],
                send_sem=send_sem,
                recv_sem=recv_sem,
                device_id={axis: lax.rem(me + off, count)},
                device_id_type=pl.DeviceIdType.MESH,
            ).start()

    def wait_bytes(buf, count, sem):
        view = buf.at[pl.ds(0, count - 1)]
        pltpu.make_async_copy(view, view, sem).wait()

    sub = lax.broadcasted_iota(jnp.int32, (q, LANES), 0)
    loads[0].wait()
    loads[1].wait()
    own_weight = jnp.concatenate(
        [weight[pl.ds(rows_s[0, s] * q, q), :] for s in range(slots)], axis=0
    )
    own_squared = own_weight * own_weight
    own_codes = jnp.concatenate([rows_s[0, s] * q + sub for s in range(slots)], axis=0)
    idbuf[me_c, 0:mrows, :] = own_squared
    idbuf[me_c, mrows : 2 * mrows, :] = own_codes.astype(F32)
    loads[2].wait()
    own_misfit = jnp.concatenate(
        [misfit[pl.ds(rows_s[0, s] * q, q), :] for s in range(slots)], axis=0
    )

    for i in (3, 4, 5):
        loads[i].wait()
    lane = lax.broadcasted_iota(jnp.int32, (1, size), 1)
    live = [lane < kept_s[0, s] for s in range(slots)]
    hits = [[cols_s[0, s] == b for b in range(blocks)] for s in range(slots)]
    scale = scale_ref[...]

    def adjoint_blocks(field):
        sums = [jnp.zeros((1, size), F32) for _ in range(blocks)]
        for s, row in enumerate(to_rows(field, size)):
            product = nn(row.astype(BF16), tiles[s])
            product = jnp.where(live[s], product, 0.0) * scale
            for b in range(blocks):
                sums[b] = sums[b] + jnp.where(hits[s][b], product, 0.0)
        return sums

    def forward_parts(cells):
        coeffs = haar_apply(nt, [depth[b] * cells[b] for b in range(blocks)], signs[...])
        coeffs = [c * scale for c in coeffs]
        products = []
        for s in range(slots):
            picked = jnp.zeros((1, size), F32)
            for b in range(blocks):
                picked = picked + jnp.where(hits[s][b], coeffs[b], 0.0)
            picked = jnp.where(live[s], picked, 0.0).astype(BF16)
            products.append(nt(picked, tiles[s]))
        return to_lanes(products)

    def put_rows(k, sums):
        for b in range(blocks):
            rowbuf[k, me_r, b : b + 1, :] = sums[b]

    def get_rows(k):
        sums = []
        for b in range(blocks):
            acc = rowbuf[k, 0, b : b + 1, :]
            for r in range(1, n_rows):
                acc = acc + rowbuf[k, r, b : b + 1, :]
            sums.append(acc)
        back = haar_apply(nn, sums, signs[...])
        return [depth[b] * back[b] for b in range(blocks)]

    loads[6].wait()
    put_rows(0, adjoint_blocks((own_squared * own_misfit).astype(BF16).astype(F32)))
    rowbuf[0, me_r, blocks : blocks + 1, :] = jnp.zeros((1, size), F32)
    pl.semaphore_wait(barrier, n_cols + n_rows - 2)
    send(rowbuf.at[0], "rows", me_r, n_rows, row_send.at[0], row_recv.at[0])
    send(idbuf, "cols", me_c, n_cols, id_send.at[0], id_recv.at[0])
    for i in (7, 8, 9):
        loads[i].wait()
    depth = to_rows(depth_ref[...], size)
    density = to_rows(density_ref[...], size)

    wait_bytes(rowbuf.at[0], n_rows, row_recv.at[0])
    adj = get_rows(0)
    residual = [adj[b] - DAMPING * density[b] for b in range(blocks)]
    direction = None
    solved = None
    norm_prev = dd = None
    parts_dir = image = change = None
    squared = codes = None

    for k in range(ITERS):
        rr_part = total([residual[b] * residual[b] for b in range(blocks)])
        colbuf[k, me_c, mrows : mrows + 1, :] = jnp.broadcast_to(rr_part, (1, LANES))
        if k:
            rd_part = total([residual[b] * direction[b] for b in range(blocks)])
            colbuf[k, me_c, mrows + 1 : mrows + 2, :] = jnp.broadcast_to(rd_part, (1, LANES))
        else:
            colbuf[k, me_c, mrows + 1 : mrows + 2, :] = jnp.zeros((1, LANES), F32)
        colbuf[k, me_c, 0:mrows, :] = forward_parts(residual)
        send(colbuf.at[k], "cols", me_c, n_cols, col_send.at[k], col_recv.at[k])
        if k == 0:
            wait_bytes(idbuf, n_cols, id_recv.at[0])
            codes = idbuf[:, mrows : 2 * mrows, :].reshape(n, LANES)
            squared = idbuf[:, 0:mrows, :].reshape(n, LANES)
            codes_row = jnp.transpose(codes)[0:1, :]
            match_ref[...] = (codes[:, 0:1] == codes_row).astype(F32).astype(BF16)
        wait_bytes(colbuf.at[k], n_cols, col_recv.at[k])
        parts = colbuf[k, :, 0:mrows, :].reshape(n, LANES)
        norm = colbuf[k, 0, mrows : mrows + 1, :]
        cross = colbuf[k, 0, mrows + 1 : mrows + 2, :]
        for c in range(1, n_cols):
            norm = norm + colbuf[k, c, mrows : mrows + 1, :]
            cross = cross + colbuf[k, c, mrows + 1 : mrows + 2, :]
        new_image = select_dot(match_ref[...], parts)
        if k == 0:
            parts_dir, image = parts, new_image
            direction = residual
            dd = norm
        else:
            beta = norm / norm_prev
            beta_row = jnp.concatenate([beta] * q, axis=1)
            parts_dir = parts + beta * parts_dir
            image = new_image + beta * image
            direction = [residual[b] + beta_row * direction[b] for b in range(blocks)]
            dd = norm + 2.0 * beta * cross + beta * beta * dd
        norm_prev = norm
        curv_part = jnp.sum(
            jnp.sum(parts_dir * (squared * image), axis=0, keepdims=True), axis=1, keepdims=True
        )
        if k + 1 < ITERS:
            image_ref[...] = image
            own_image = image_ref[pl.ds(pl.multiple_of(me_c * mrows, mrows), mrows), :]
            put_rows(k + 1, adjoint_blocks(own_squared * own_image))
            rowbuf[k + 1, me_r, blocks : blocks + 1, :] = jnp.broadcast_to(curv_part, (1, size))
            send(rowbuf.at[k + 1], "rows", me_r, n_rows, row_send.at[k + 1], row_recv.at[k + 1])
            wait_bytes(rowbuf.at[k + 1], n_rows, row_recv.at[k + 1])
            curv = rowbuf[k + 1, 0, blocks : blocks + 1, 0:LANES]
            for r in range(1, n_rows):
                curv = curv + rowbuf[k + 1, r, blocks : blocks + 1, 0:LANES]
        else:
            curvbuf[me_r, :, :] = jnp.broadcast_to(curv_part, (8, LANES))
            send(curvbuf, "rows", me_r, n_rows, curv_send.at[0], curv_recv.at[0])
            wait_bytes(curvbuf, n_rows, curv_recv.at[0])
            curv = curvbuf[0, 0:1, :]
            for r in range(1, n_rows):
                curv = curv + curvbuf[r, 0:1, :]
        alpha = norm / (curv + DAMPING * dd)
        alpha_row = jnp.concatenate([alpha] * q, axis=1)
        if k == 0:
            solved = [alpha_row * direction[b] for b in range(blocks)]
            change = alpha * parts_dir
        else:
            solved = [solved[b] + alpha_row * direction[b] for b in range(blocks)]
            change = change + alpha * parts_dir
        if k + 1 < ITERS:
            adj = get_rows(k + 1)
            residual = [
                residual[b] - alpha_row * (adj[b] + DAMPING * direction[b]) for b in range(blocks)
            ]

    density_out[...] = to_lanes([density[b] + depth[b] * solved[b] for b in range(blocks)])
    share = misfit_out.shape[0]
    wanted = (lax.broadcasted_iota(jnp.int32, (share, n), 0) + me_c * share).astype(F32)
    pick = (wanted == jnp.transpose(codes)[0:1, :]).astype(F32).astype(BF16)
    own_share = misfit[pl.ds(pl.multiple_of(me_c * share, 8), share), :]
    misfit_out[...] = own_share - select_dot(pick, change)

    wait_bytes(idbuf, n_cols, id_send.at[0])
    wait_bytes(curvbuf, n_rows, curv_send.at[0])
    for k in range(ITERS):
        wait_bytes(colbuf.at[k], n_cols, col_send.at[k])
        wait_bytes(rowbuf.at[k], n_rows, row_send.at[k])


def per_device(
    n_rows, n_cols,
    sensitivity, tile_rows, tile_cols, kept_counts, misfit, data_weight, depth_weight, density
):
    slots, size = sensitivity.shape[1], sensitivity.shape[-1]
    q = size // LANES
    data_lanes = misfit.shape[0] // LANES
    cell_lanes = density.shape[0] // LANES
    blocks = density.shape[0] // size
    share = data_lanes // n_cols
    mrows = slots * q
    n = n_cols * mrows
    signs, scale = haar_signs(size)
    vmem = pl.BlockSpec(memory_space=pltpu.VMEM)
    hbm = pl.BlockSpec(memory_space=pltpu.HBM)
    dma = pltpu.SemaphoreType.DMA
    new_density, new_misfit = pl.pallas_call(
        functools.partial(kernel, n_rows, n_cols, slots),
        out_shape=(
            jax.ShapeDtypeStruct((cell_lanes, LANES), F32),
            jax.ShapeDtypeStruct((share, LANES), F32),
        ),
        in_specs=[hbm] * 10,
        out_specs=(vmem, vmem),
        scratch_shapes=[
            pltpu.SMEM((1, slots), jnp.int32),
            pltpu.SMEM((1, slots), jnp.int32),
            pltpu.SMEM((1, slots), jnp.int32),
            pltpu.VMEM((1, size), F32),
            pltpu.VMEM((cell_lanes, LANES), F32),
            pltpu.VMEM((cell_lanes, LANES), F32),
            pltpu.VMEM((slots, size, size), BF16),
            pltpu.VMEM((size, size), BF16),
            pltpu.VMEM((data_lanes, LANES), F32),
            pltpu.VMEM((data_lanes, LANES), F32),
            pltpu.VMEM((n_cols, 2 * mrows, LANES), F32),
            pltpu.VMEM((ITERS, n_cols, mrows + 8, LANES), F32),
            pltpu.VMEM((ITERS, n_rows, blocks + 2, size), F32),
            pltpu.VMEM((n_rows, 8, LANES), F32),
            pltpu.VMEM((n, LANES), F32),
            pltpu.VMEM((n, n), BF16),
            dma((10,)), dma((1,)), dma((1,)), dma((ITERS,)), dma((ITERS,)),
            dma((ITERS,)), dma((ITERS,)), dma((1,)), dma((1,)),
        ],
        compiler_params=pltpu.CompilerParams(
            collective_id=0, has_side_effects=True, vmem_limit_bytes=67_043_328
        ),
    )(
        tile_rows, tile_cols, kept_counts, jnp.asarray(scale),
        depth_weight.reshape(cell_lanes, LANES), density.reshape(cell_lanes, LANES),
        sensitivity[0], jnp.asarray(signs, BF16),
        misfit.reshape(data_lanes, LANES), data_weight.reshape(data_lanes, LANES),
    )
    return new_density.reshape(-1), new_misfit.reshape(-1)


def solution(mesh):
    return jax.shard_map(
        functools.partial(per_device, mesh.shape["rows"], mesh.shape["cols"]),
        mesh=mesh,
        in_specs=(
            P("rows", "cols", None, None),
            P("rows", "cols"),
            P("rows", "cols"),
            P("rows", "cols"),
            P("rows"),
            P("rows"),
            P("cols"),
            P("cols"),
        ),
        out_specs=(P("cols"), P(("rows", "cols"))),
        check_vma=False,
    )
```

```python
import functools
import math

import jax
import jax.numpy as jnp
import numpy as np
from jax import lax
from jax.experimental import pallas as pl
from jax.experimental.pallas import tpu as pltpu
from jax.sharding import PartitionSpec as P

ITERS = 4
DAMPING = 1.0
LANES = 128
F32 = jnp.float32
BF16 = jnp.bfloat16


def haar_signs(size):
    signs = np.zeros((size, size), np.float32)
    scale = np.zeros((1, size), np.float32)
    signs[0] = 1.0
    scale[0, 0] = 1.0 / math.sqrt(size)
    for n in range(1, size):
        level = n.bit_length() - 1
        k = n - (1 << level)
        support = size >> level
        signs[n, k * support : k * support + support // 2] = 1.0
        signs[n, k * support + support // 2 : (k + 1) * support] = -1.0
        scale[0, n] = 1.0 / math.sqrt(support)
    return signs, scale


def split3(x):
    hi = x.astype(BF16)
    rest = x - hi.astype(F32)
    mid = rest.astype(BF16)
    low = (rest - mid.astype(F32)).astype(BF16)
    return hi, mid, low


def nn(a, b):
    return lax.dot_general(a, b, (((1,), (0,)), ((), ())), preferred_element_type=F32)


def nt(a, b):
    return lax.dot_general(a, b, (((1,), (1,)), ((), ())), preferred_element_type=F32)


def select_dot(sel, x):
    hi, mid, low = split3(x)
    return nn(sel, hi) + (nn(sel, mid) + nn(sel, low))


def to_rows(x, width):
    q = width // LANES
    return [
        jnp.concatenate([x[i * q + j : i * q + j + 1, :] for j in range(q)], axis=1)
        for i in range(x.shape[0] // q)
    ]


def to_lanes(rows):
    q = rows[0].shape[1] // LANES
    return jnp.concatenate(
        [row[:, j * LANES : (j + 1) * LANES] for row in rows for j in range(q)], axis=0
    )


def haar_apply(dot, rows, matrix):
    m = len(rows)
    parts = [split3(row) for row in rows]
    lhs = jnp.concatenate([p[t].astype(F32) for t in range(3) for p in parts], axis=0).astype(BF16)
    out = dot(lhs, matrix)
    return [out[i : i + 1] + (out[m + i : m + i + 1] + out[2 * m + i : 2 * m + i + 1]) for i in range(m)]


def total(rows):
    acc = rows[0]
    for row in rows[1:]:
        acc = acc + row
    return jnp.sum(acc, axis=1, keepdims=True)


def kernel(
    n_rows, n_cols, slots,
    rows_hbm, cols_hbm, kept_hbm, scale_hbm, depth_hbm, density_hbm,
    tiles_hbm, signs_hbm, misfit_hbm, weight_hbm,
    density_out, misfit_out,
    rows_s, cols_s, kept_s, scale_ref, depth_ref, density_ref,
    tiles, signs, misfit, weight,
    idbuf, colbuf, dotbuf, rowbuf, curvbuf, image_ref, match_ref,
    load_sem, id_send, id_recv, col_send, col_recv, dot_send, dot_recv,
    row_send, row_recv, curv_send, curv_recv,
):
    size = tiles.shape[-1]
    q = size // LANES
    blocks = depth_ref.shape[0] * LANES // size
    mrows = slots * q
    n = n_cols * mrows
    me_r = lax.axis_index("rows")
    me_c = lax.axis_index("cols")

    loads = [
        pltpu.make_async_copy(src, dst, load_sem.at[i])
        for i, (src, dst) in enumerate(
            (
                (rows_hbm, rows_s), (weight_hbm, weight), (misfit_hbm, misfit),
                (kept_hbm, kept_s), (cols_hbm, cols_s), (scale_hbm, scale_ref),
                (tiles_hbm, tiles), (signs_hbm, signs),
                (depth_hbm, depth_ref), (density_hbm, density_ref),
            )
        )
    ]
    for load in loads:
        load.start()

    barrier = pltpu.get_barrier_semaphore()
    for off in range(1, n_cols):
        pl.semaphore_signal(
            barrier, inc=1, device_id={"cols": lax.rem(me_c + off, n_cols)},
            device_id_type=pl.DeviceIdType.MESH,
        )
    for off in range(1, n_rows):
        pl.semaphore_signal(
            barrier, inc=1, device_id={"rows": lax.rem(me_r + off, n_rows)},
            device_id_type=pl.DeviceIdType.MESH,
        )

    def far_first(me, count):
        upper = (2 * me) // count
        for j in range(count - 1):
            down = count - 1 - j
            down = down - lax.select(down <= me, 1, 0)
            up = j + lax.select(j >= me, 1, 0)
            yield down + upper * (up - down)

    def send(buf, axis, me, count, send_sem, recv_sem):
        for peer in far_first(me, count):
            pltpu.make_async_remote_copy(
                src_ref=buf.at[me],
                dst_ref=buf.at[me],
                send_sem=send_sem,
                recv_sem=recv_sem,
                device_id={axis: peer},
                device_id_type=pl.DeviceIdType.MESH,
            ).start()

    def wait_bytes(buf, count, sem):
        view = buf.at[pl.ds(0, count - 1)]
        pltpu.make_async_copy(view, view, sem).wait()

    sub = lax.broadcasted_iota(jnp.int32, (q, LANES), 0)
    loads[0].wait()
    loads[1].wait()
    own_weight = jnp.concatenate(
        [weight[pl.ds(rows_s[0, s] * q, q), :] for s in range(slots)], axis=0
    )
    own_squared = own_weight * own_weight
    own_codes = jnp.concatenate([rows_s[0, s] * q + sub for s in range(slots)], axis=0)
    idbuf[me_c, 0:mrows, :] = own_squared
    idbuf[me_c, mrows : 2 * mrows, :] = own_codes.astype(F32)
    loads[2].wait()
    own_misfit = jnp.concatenate(
        [misfit[pl.ds(rows_s[0, s] * q, q), :] for s in range(slots)], axis=0
    )

    for i in (3, 4, 5):
        loads[i].wait()
    lane = lax.broadcasted_iota(jnp.int32, (1, size), 1)
    live = [lane < kept_s[0, s] for s in range(slots)]
    hits = [[cols_s[0, s] == b for b in range(blocks)] for s in range(slots)]
    scale = scale_ref[...]

    def adjoint_blocks(field):
        sums = [jnp.zeros((1, size), F32) for _ in range(blocks)]
        for s, row in enumerate(to_rows(field, size)):
            product = nn(row.astype(BF16), tiles[s])
            product = jnp.where(live[s], product, 0.0) * scale
            for b in range(blocks):
                sums[b] = sums[b] + jnp.where(hits[s][b], product, 0.0)
        return sums

    def forward_parts(cells):
        coeffs = haar_apply(nt, [depth[b] * cells[b] for b in range(blocks)], signs[...])
        coeffs = [c * scale for c in coeffs]
        products = []
        for s in range(slots):
            picked = jnp.zeros((1, size), F32)
            for b in range(blocks):
                picked = picked + jnp.where(hits[s][b], coeffs[b], 0.0)
            picked = jnp.where(live[s], picked, 0.0).astype(BF16)
            products.append(nt(picked, tiles[s]))
        return to_lanes(products)

    def put_rows(k, sums):
        for b in range(blocks):
            rowbuf[k, me_r, b : b + 1, :] = sums[b]

    def get_rows(k):
        sums = []
        for b in range(blocks):
            acc = rowbuf[k, 0, b : b + 1, :]
            for r in range(1, n_rows):
                acc = acc + rowbuf[k, r, b : b + 1, :]
            sums.append(acc)
        back = haar_apply(nn, sums, signs[...])
        return [depth[b] * back[b] for b in range(blocks)]

    loads[6].wait()
    put_rows(0, adjoint_blocks((own_squared * own_misfit).astype(BF16).astype(F32)))
    pl.semaphore_wait(barrier, n_cols + n_rows - 2)
    send(rowbuf.at[0], "rows", me_r, n_rows, row_send.at[0], row_recv.at[0])
    send(idbuf, "cols", me_c, n_cols, id_send.at[0], id_recv.at[0])
    for i in (7, 8, 9):
        loads[i].wait()
    depth = to_rows(depth_ref[...], size)
    density = to_rows(density_ref[...], size)

    wait_bytes(rowbuf.at[0], n_rows, row_recv.at[0])
    adj = get_rows(0)
    residual = [adj[b] - DAMPING * density[b] for b in range(blocks)]
    direction = None
    solved = None
    norm_prev = dd = None
    parts_dir = image = change = None
    squared = codes = None

    for k in range(ITERS):
        dots = [total([residual[b] * residual[b] for b in range(blocks)])]
        if k:
            dots.append(total([residual[b] * direction[b] for b in range(blocks)]))
        else:
            dots.append(jnp.zeros((1, 1), F32))
        for i in range(2):
            dotbuf[k, me_c, i : i + 1, :] = jnp.broadcast_to(dots[i], (1, LANES))
        send(dotbuf.at[k], "cols", me_c, n_cols, dot_send.at[k], dot_recv.at[k])
        colbuf[k, me_c, :, :] = forward_parts(residual).astype(BF16)
        send(colbuf.at[k], "cols", me_c, n_cols, col_send.at[k], col_recv.at[k])
        if k == 0:
            wait_bytes(idbuf, n_cols, id_recv.at[0])
            codes = idbuf[:, mrows : 2 * mrows, :].reshape(n, LANES)
            squared = idbuf[:, 0:mrows, :].reshape(n, LANES)
            codes_row = jnp.transpose(codes)[0:1, :]
            match_ref[...] = (codes[:, 0:1] == codes_row).astype(F32).astype(BF16)
        wait_bytes(dotbuf.at[k], n_cols, dot_recv.at[k])
        norm = dotbuf[k, 0, 0:1, :]
        cross = dotbuf[k, 0, 1:2, :]
        for c in range(1, n_cols):
            norm = norm + dotbuf[k, c, 0:1, :]
            cross = cross + dotbuf[k, c, 1:2, :]
        wait_bytes(colbuf.at[k], n_cols, col_recv.at[k])
        parts = colbuf[k].reshape(n, LANES)
        new_image = nn(match_ref[...], parts)
        parts = parts.astype(F32)
        if k == 0:
            parts_dir, image = parts, new_image
            direction = residual
            dd = norm
        else:
            beta = norm / norm_prev
            beta_row = jnp.concatenate([beta] * q, axis=1)
            parts_dir = parts + beta * parts_dir
            image = new_image + beta * image
            direction = [residual[b] + beta_row * direction[b] for b in range(blocks)]
            dd = norm + 2.0 * beta * cross + beta * beta * dd
        norm_prev = norm
        curv_part = jnp.sum(
            jnp.sum(parts_dir * (squared * image), axis=0, keepdims=True), axis=1, keepdims=True
        )
        if k + 1 < ITERS:
            image_ref[...] = image
            own_image = image_ref[pl.ds(pl.multiple_of(me_c * mrows, mrows), mrows), :]
            put_rows(k + 1, adjoint_blocks(own_squared * own_image))
            send(rowbuf.at[k + 1], "rows", me_r, n_rows, row_send.at[k + 1], row_recv.at[k + 1])
        curvbuf[k, me_r, :, :] = jnp.broadcast_to(curv_part, (1, LANES))
        send(curvbuf.at[k], "rows", me_r, n_rows, curv_send.at[k], curv_recv.at[k])
        if k + 1 < ITERS:
            wait_bytes(rowbuf.at[k + 1], n_rows, row_recv.at[k + 1])
            adj = get_rows(k + 1)
        wait_bytes(curvbuf.at[k], n_rows, curv_recv.at[k])
        curv = curvbuf[k, 0, 0:1, :]
        for r in range(1, n_rows):
            curv = curv + curvbuf[k, r, 0:1, :]
        alpha = norm / (curv + DAMPING * dd)
        alpha_row = jnp.concatenate([alpha] * q, axis=1)
        if k == 0:
            solved = [alpha_row * direction[b] for b in range(blocks)]
            change = alpha * parts_dir
        else:
            solved = [solved[b] + alpha_row * direction[b] for b in range(blocks)]
            change = change + alpha * parts_dir
        if k + 1 < ITERS:
            residual = [
                residual[b] - alpha_row * (adj[b] + DAMPING * direction[b]) for b in range(blocks)
            ]

    density_out[...] = to_lanes([density[b] + depth[b] * solved[b] for b in range(blocks)])
    share = misfit_out.shape[0]
    wanted = (lax.broadcasted_iota(jnp.int32, (share, n), 0) + me_c * share).astype(F32)
    pick = (wanted == jnp.transpose(codes)[0:1, :]).astype(F32).astype(BF16)
    own_share = misfit[pl.ds(pl.multiple_of(me_c * share, 8), share), :]
    misfit_out[...] = own_share - select_dot(pick, change)

    wait_bytes(idbuf, n_cols, id_send.at[0])
    for k in range(ITERS):
        wait_bytes(colbuf.at[k], n_cols, col_send.at[k])
        wait_bytes(dotbuf.at[k], n_cols, dot_send.at[k])
        wait_bytes(rowbuf.at[k], n_rows, row_send.at[k])
        wait_bytes(curvbuf.at[k], n_rows, curv_send.at[k])


def per_device(
    n_rows, n_cols,
    sensitivity, tile_rows, tile_cols, kept_counts, misfit, data_weight, depth_weight, density
):
    slots, size = sensitivity.shape[1], sensitivity.shape[-1]
    q = size // LANES
    data_lanes = misfit.shape[0] // LANES
    cell_lanes = density.shape[0] // LANES
    blocks = density.shape[0] // size
    share = data_lanes // n_cols
    mrows = slots * q
    n = n_cols * mrows
    signs, scale = haar_signs(size)
    vmem = pl.BlockSpec(memory_space=pltpu.VMEM)
    hbm = pl.BlockSpec(memory_space=pltpu.HBM)
    dma = pltpu.SemaphoreType.DMA
    new_density, new_misfit = pl.pallas_call(
        functools.partial(kernel, n_rows, n_cols, slots),
        out_shape=(
            jax.ShapeDtypeStruct((cell_lanes, LANES), F32),
            jax.ShapeDtypeStruct((share, LANES), F32),
        ),
        in_specs=[hbm] * 10,
        out_specs=(vmem, vmem),
        scratch_shapes=[
            pltpu.SMEM((1, slots), jnp.int32),
            pltpu.SMEM((1, slots), jnp.int32),
            pltpu.SMEM((1, slots), jnp.int32),
            pltpu.VMEM((1, size), F32),
            pltpu.VMEM((cell_lanes, LANES), F32),
            pltpu.VMEM((cell_lanes, LANES), F32),
            pltpu.VMEM((slots, size, size), BF16),
            pltpu.VMEM((size, size), BF16),
            pltpu.VMEM((data_lanes, LANES), F32),
            pltpu.VMEM((data_lanes, LANES), F32),
            pltpu.VMEM((n_cols, 2 * mrows, LANES), F32),
            pltpu.VMEM((ITERS, n_cols, mrows, LANES), BF16),
            pltpu.VMEM((ITERS, n_cols, 2, LANES), F32),
            pltpu.VMEM((ITERS, n_rows, blocks, size), F32),
            pltpu.VMEM((ITERS, n_rows, 1, LANES), F32),
            pltpu.VMEM((n, LANES), F32),
            pltpu.VMEM((n, n), BF16),
            dma((10,)), dma((1,)), dma((1,)), dma((ITERS,)), dma((ITERS,)),
            dma((ITERS,)), dma((ITERS,)), dma((ITERS,)), dma((ITERS,)), dma((ITERS,)), dma((ITERS,)),
        ],
        compiler_params=pltpu.CompilerParams(
            collective_id=0, has_side_effects=True, vmem_limit_bytes=67_043_328
        ),
    )(
        tile_rows, tile_cols, kept_counts, jnp.asarray(scale),
        depth_weight.reshape(cell_lanes, LANES), density.reshape(cell_lanes, LANES),
        sensitivity[0], jnp.asarray(signs, BF16),
        misfit.reshape(data_lanes, LANES), data_weight.reshape(data_lanes, LANES),
    )
    return new_density.reshape(-1), new_misfit.reshape(-1)


def solution(mesh):
    return jax.shard_map(
        functools.partial(per_device, mesh.shape["rows"], mesh.shape["cols"]),
        mesh=mesh,
        in_specs=(
            P("rows", "cols", None, None),
            P("rows", "cols"),
            P("rows", "cols"),
            P("rows", "cols"),
            P("rows"),
            P("rows"),
            P("cols"),
            P("cols"),
        ),
        out_specs=(P("cols"), P(("rows", "cols"))),
        check_vma=False,
    )
```

```python
import functools
import math

import jax
import jax.numpy as jnp
import numpy as np
from jax import lax
from jax.experimental import pallas as pl
from jax.experimental.pallas import tpu as pltpu
from jax.sharding import PartitionSpec as P

ITERS = 4
DAMPING = 1.0
LANES = 128
F32 = jnp.float32
BF16 = jnp.bfloat16


def haar_matrix(size):
    matrix = np.zeros((size, size), np.float32)
    matrix[0] = 1.0 / math.sqrt(size)
    for n in range(1, size):
        level = n.bit_length() - 1
        k = n - (1 << level)
        support = size >> level
        value = 1.0 / math.sqrt(support)
        matrix[n, k * support : k * support + support // 2] = value
        matrix[n, k * support + support // 2 : (k + 1) * support] = -value
    high = matrix.astype(BF16)
    low = (matrix - high.astype(np.float32)).astype(BF16)
    return high, low


def split3(x):
    hi = x.astype(BF16)
    rest = x - hi.astype(F32)
    mid = rest.astype(BF16)
    low = (rest - mid.astype(F32)).astype(BF16)
    return hi, mid, low


def nn(a, b):
    return lax.dot_general(a, b, (((1,), (0,)), ((), ())), preferred_element_type=F32)


def nt(a, b):
    return lax.dot_general(a, b, (((1,), (1,)), ((), ())), preferred_element_type=F32)


def select_dot(sel, x):
    hi, mid, low = split3(x)
    return nn(sel, hi) + (nn(sel, mid) + nn(sel, low))


def to_rows(x, width):
    q = width // LANES
    return [
        jnp.concatenate([x[i * q + j : i * q + j + 1, :] for j in range(q)], axis=1)
        for i in range(x.shape[0] // q)
    ]


def to_lanes(rows):
    q = rows[0].shape[1] // LANES
    return jnp.concatenate(
        [row[:, j * LANES : (j + 1) * LANES] for row in rows for j in range(q)], axis=0
    )


def total(rows):
    acc = rows[0]
    for row in rows[1:]:
        acc = acc + row
    return jnp.sum(acc, axis=1, keepdims=True)


def kernel(
    n_rows, n_cols, slots,
    rows_hbm, cols_hbm, kept_hbm, depth_hbm, density_hbm,
    tiles_hbm, high_hbm, low_hbm, misfit_hbm, weight_hbm,
    density_out, misfit_out,
    rows_s, cols_s, kept_s, depth_ref, density_ref,
    tiles, high, low, misfit, weight,
    idbuf, colbuf, dotbuf, rowbuf, curvbuf, image_ref, match_ref,
    load_sem, id_send, id_recv, col_send, col_recv, dot_send, dot_recv,
    row_send, row_recv, curv_send, curv_recv,
):
    size = tiles.shape[-1]
    q = size // LANES
    blocks = depth_ref.shape[0] * LANES // size
    mrows = slots * q
    n = n_cols * mrows
    me_r = lax.axis_index("rows")
    me_c = lax.axis_index("cols")

    loads = [
        pltpu.make_async_copy(src, dst, load_sem.at[i])
        for i, (src, dst) in enumerate(
            (
                (kept_hbm, kept_s), (cols_hbm, cols_s), (rows_hbm, rows_s), (depth_hbm, depth_ref),
                (tiles_hbm, tiles), (high_hbm, high), (low_hbm, low),
                (weight_hbm, weight), (misfit_hbm, misfit), (density_hbm, density_ref),
            )
        )
    ]
    for load in loads:
        load.start()

    barrier = pltpu.get_barrier_semaphore()
    for off in range(1, n_cols):
        pl.semaphore_signal(
            barrier, inc=1, device_id={"cols": lax.rem(me_c + off, n_cols)},
            device_id_type=pl.DeviceIdType.MESH,
        )
    for off in range(1, n_rows):
        pl.semaphore_signal(
            barrier, inc=1, device_id={"rows": lax.rem(me_r + off, n_rows)},
            device_id_type=pl.DeviceIdType.MESH,
        )

    def far_first(me, count):
        upper = (2 * me) // count
        for j in range(count - 1):
            down = count - 1 - j
            down = down - lax.select(down <= me, 1, 0)
            up = j + lax.select(j >= me, 1, 0)
            yield down + upper * (up - down)

    def send(buf, axis, me, count, send_sem, recv_sem):
        for peer in far_first(me, count):
            pltpu.make_async_remote_copy(
                src_ref=buf.at[me],
                dst_ref=buf.at[me],
                send_sem=send_sem,
                recv_sem=recv_sem,
                device_id={axis: peer},
                device_id_type=pl.DeviceIdType.MESH,
            ).start()

    def wait_bytes(buf, count, sem):
        view = buf.at[pl.ds(0, count - 1)]
        pltpu.make_async_copy(view, view, sem).wait()

    for load in loads:
        load.wait()
    sub = lax.broadcasted_iota(jnp.int32, (q, LANES), 0)
    own_weight = jnp.concatenate(
        [weight[pl.ds(rows_s[0, s] * q, q), :] for s in range(slots)], axis=0
    )
    own_squared = own_weight * own_weight
    own_codes = jnp.concatenate([rows_s[0, s] * q + sub for s in range(slots)], axis=0)
    idbuf[me_c, 0:mrows, :] = own_squared
    idbuf[me_c, mrows : 2 * mrows, :] = own_codes.astype(F32)
    own_misfit = jnp.concatenate(
        [misfit[pl.ds(rows_s[0, s] * q, q), :] for s in range(slots)], axis=0
    )

    lane = lax.broadcasted_iota(jnp.int32, (1, size), 1)
    hits = [[cols_s[0, s] == b for b in range(blocks)] for s in range(slots)]
    depth = to_rows(depth_ref[...], size)
    density = to_rows(density_ref[...], size)

    for s in range(slots):
        live = jnp.where(lane < kept_s[0, s], 1.0, 0.0).astype(BF16)
        masked = tiles[s] * live
        cell_weight = jnp.zeros((1, size), F32)
        for b in range(blocks):
            cell_weight = cell_weight + jnp.where(hits[s][b], depth[b], 0.0)
        tiles[s] = ((nn(masked, high[...]) + nn(masked, low[...])) * cell_weight).astype(BF16)

    def adjoint_blocks(field):
        sums = [jnp.zeros((1, size), F32) for _ in range(blocks)]
        for s, row in enumerate(to_rows(field, size)):
            product = nn(row.astype(BF16), tiles[s])
            for b in range(blocks):
                sums[b] = sums[b] + jnp.where(hits[s][b], product, 0.0)
        return sums

    def forward_parts(cells):
        products = []
        for s in range(slots):
            picked = jnp.zeros((1, size), F32)
            for b in range(blocks):
                picked = picked + jnp.where(hits[s][b], cells[b], 0.0)
            products.append(nt(picked.astype(BF16), tiles[s]))
        return to_lanes(products)

    def put_rows(k, sums):
        for b in range(blocks):
            rowbuf[k, me_r, b : b + 1, :] = sums[b]

    def get_rows(k):
        sums = []
        for b in range(blocks):
            acc = rowbuf[k, 0, b : b + 1, :]
            for r in range(1, n_rows):
                acc = acc + rowbuf[k, r, b : b + 1, :]
            sums.append(acc)
        return sums

    put_rows(0, adjoint_blocks((own_squared * own_misfit).astype(BF16).astype(F32)))
    pl.semaphore_wait(barrier, n_cols + n_rows - 2)
    send(rowbuf.at[0], "rows", me_r, n_rows, row_send.at[0], row_recv.at[0])
    send(idbuf, "cols", me_c, n_cols, id_send.at[0], id_recv.at[0])
    wait_bytes(rowbuf.at[0], n_rows, row_recv.at[0])
    adj = get_rows(0)
    residual = [adj[b] - DAMPING * density[b] for b in range(blocks)]
    direction = None
    solved = None
    norm_prev = dd = None
    parts_dir = image = change = None
    squared = codes = None

    for k in range(ITERS):
        dots = [total([residual[b] * residual[b] for b in range(blocks)])]
        if k:
            dots.append(total([residual[b] * direction[b] for b in range(blocks)]))
        else:
            dots.append(jnp.zeros((1, 1), F32))
        for i in range(2):
            dotbuf[k, me_c, i : i + 1, :] = jnp.broadcast_to(dots[i], (1, LANES))
        send(dotbuf.at[k], "cols", me_c, n_cols, dot_send.at[k], dot_recv.at[k])
        colbuf[k, me_c, :, :] = forward_parts(residual).astype(BF16)
        send(colbuf.at[k], "cols", me_c, n_cols, col_send.at[k], col_recv.at[k])
        if k == 0:
            wait_bytes(idbuf, n_cols, id_recv.at[0])
            codes = idbuf[:, mrows : 2 * mrows, :].reshape(n, LANES)
            squared = idbuf[:, 0:mrows, :].reshape(n, LANES)
            codes_row = jnp.transpose(codes)[0:1, :]
            match_ref[...] = (codes[:, 0:1] == codes_row).astype(F32).astype(BF16)
        wait_bytes(dotbuf.at[k], n_cols, dot_recv.at[k])
        norm = dotbuf[k, 0, 0:1, :]
        cross = dotbuf[k, 0, 1:2, :]
        for c in range(1, n_cols):
            norm = norm + dotbuf[k, c, 0:1, :]
            cross = cross + dotbuf[k, c, 1:2, :]
        wait_bytes(colbuf.at[k], n_cols, col_recv.at[k])
        parts = colbuf[k].reshape(n, LANES)
        new_image = nn(match_ref[...], parts)
        parts = parts.astype(F32)
        if k == 0:
            parts_dir, image = parts, new_image
            direction = residual
            dd = norm
        else:
            beta = norm / norm_prev
            beta_row = jnp.concatenate([beta] * q, axis=1)
            parts_dir = parts + beta * parts_dir
            image = new_image + beta * image
            direction = [residual[b] + beta_row * direction[b] for b in range(blocks)]
            dd = norm + 2.0 * beta * cross + beta * beta * dd
        norm_prev = norm
        curv_part = jnp.sum(
            jnp.sum(parts_dir * (squared * image), axis=0, keepdims=True), axis=1, keepdims=True
        )
        if k + 1 < ITERS:
            image_ref[...] = image
            own_image = image_ref[pl.ds(pl.multiple_of(me_c * mrows, mrows), mrows), :]
            put_rows(k + 1, adjoint_blocks(own_squared * own_image))
            send(rowbuf.at[k + 1], "rows", me_r, n_rows, row_send.at[k + 1], row_recv.at[k + 1])
        curvbuf[k, me_r, :, :] = jnp.broadcast_to(curv_part, (1, LANES))
        send(curvbuf.at[k], "rows", me_r, n_rows, curv_send.at[k], curv_recv.at[k])
        if k + 1 == ITERS:
            share = misfit_out.shape[0]
            wanted = (lax.broadcasted_iota(jnp.int32, (share, n), 0) + me_c * share).astype(F32)
            pick = (wanted == jnp.transpose(codes)[0:1, :]).astype(F32).astype(BF16)
            own_share = misfit[pl.ds(pl.multiple_of(me_c * share, 8), share), :]
            own_share = own_share - select_dot(pick, change)
            last_share = select_dot(pick, parts_dir)
        if k + 1 < ITERS:
            wait_bytes(rowbuf.at[k + 1], n_rows, row_recv.at[k + 1])
            adj = get_rows(k + 1)
        wait_bytes(curvbuf.at[k], n_rows, curv_recv.at[k])
        curv = curvbuf[k, 0, 0:1, :]
        for r in range(1, n_rows):
            curv = curv + curvbuf[k, r, 0:1, :]
        alpha = norm / (curv + DAMPING * dd)
        alpha_row = jnp.concatenate([alpha] * q, axis=1)
        if k == 0:
            solved = [alpha_row * direction[b] for b in range(blocks)]
            change = alpha * parts_dir
        else:
            solved = [solved[b] + alpha_row * direction[b] for b in range(blocks)]
            if k + 1 < ITERS:
                change = change + alpha * parts_dir
        if k + 1 < ITERS:
            residual = [
                residual[b] - alpha_row * (adj[b] + DAMPING * direction[b]) for b in range(blocks)
            ]

    density_out[...] = to_lanes([density[b] + depth[b] * solved[b] for b in range(blocks)])
    misfit_out[...] = own_share - alpha * last_share

    wait_bytes(idbuf, n_cols, id_send.at[0])
    for k in range(ITERS):
        wait_bytes(colbuf.at[k], n_cols, col_send.at[k])
        wait_bytes(dotbuf.at[k], n_cols, dot_send.at[k])
        wait_bytes(rowbuf.at[k], n_rows, row_send.at[k])
        wait_bytes(curvbuf.at[k], n_rows, curv_send.at[k])


def per_device(
    n_rows, n_cols,
    sensitivity, tile_rows, tile_cols, kept_counts, misfit, data_weight, depth_weight, density
):
    slots, size = sensitivity.shape[1], sensitivity.shape[-1]
    q = size // LANES
    data_lanes = misfit.shape[0] // LANES
    cell_lanes = density.shape[0] // LANES
    blocks = density.shape[0] // size
    share = data_lanes // n_cols
    mrows = slots * q
    n = n_cols * mrows
    high, low = haar_matrix(size)
    vmem = pl.BlockSpec(memory_space=pltpu.VMEM)
    hbm = pl.BlockSpec(memory_space=pltpu.HBM)
    dma = pltpu.SemaphoreType.DMA
    new_density, new_misfit = pl.pallas_call(
        functools.partial(kernel, n_rows, n_cols, slots),
        out_shape=(
            jax.ShapeDtypeStruct((cell_lanes, LANES), F32),
            jax.ShapeDtypeStruct((share, LANES), F32),
        ),
        in_specs=[hbm] * 10,
        out_specs=(vmem, vmem),
        scratch_shapes=[
            pltpu.SMEM((1, slots), jnp.int32),
            pltpu.SMEM((1, slots), jnp.int32),
            pltpu.SMEM((1, slots), jnp.int32),
            pltpu.VMEM((cell_lanes, LANES), F32),
            pltpu.VMEM((cell_lanes, LANES), F32),
            pltpu.VMEM((slots, size, size), BF16),
            pltpu.VMEM((size, size), BF16),
            pltpu.VMEM((size, size), BF16),
            pltpu.VMEM((data_lanes, LANES), F32),
            pltpu.VMEM((data_lanes, LANES), F32),
            pltpu.VMEM((n_cols, 2 * mrows, LANES), F32),
            pltpu.VMEM((ITERS, n_cols, mrows, LANES), BF16),
            pltpu.VMEM((ITERS, n_cols, 2, LANES), F32),
            pltpu.VMEM((ITERS, n_rows, blocks, size), F32),
            pltpu.VMEM((ITERS, n_rows, 1, LANES), F32),
            pltpu.VMEM((n, LANES), F32),
            pltpu.VMEM((n, n), BF16),
            dma((10,)), dma((1,)), dma((1,)), dma((ITERS,)), dma((ITERS,)),
            dma((ITERS,)), dma((ITERS,)), dma((ITERS,)), dma((ITERS,)), dma((ITERS,)), dma((ITERS,)),
        ],
        compiler_params=pltpu.CompilerParams(
            collective_id=0, has_side_effects=True, vmem_limit_bytes=67_043_328
        ),
    )(
        tile_rows, tile_cols, kept_counts,
        depth_weight.reshape(cell_lanes, LANES), density.reshape(cell_lanes, LANES),
        sensitivity[0], jnp.asarray(high), jnp.asarray(low),
        misfit.reshape(data_lanes, LANES), data_weight.reshape(data_lanes, LANES),
    )
    return new_density.reshape(-1), new_misfit.reshape(-1)


def solution(mesh):
    return jax.shard_map(
        functools.partial(per_device, mesh.shape["rows"], mesh.shape["cols"]),
        mesh=mesh,
        in_specs=(
            P("rows", "cols", None, None),
            P("rows", "cols"),
            P("rows", "cols"),
            P("rows", "cols"),
            P("rows"),
            P("rows"),
            P("cols"),
            P("cols"),
        ),
        out_specs=(P("cols"), P(("rows", "cols"))),
        check_vma=False,
    )
```

```python
import functools
import math

import jax
import jax.numpy as jnp
import numpy as np
from jax import lax
from jax.experimental import pallas as pl
from jax.experimental.pallas import tpu as pltpu
from jax.sharding import PartitionSpec as P

ITERS = 4
DAMPING = 1.0
LANES = 128
F32 = jnp.float32
BF16 = jnp.bfloat16


def haar_matrix(size):
    matrix = np.zeros((size, size), np.float32)
    matrix[0] = 1.0 / math.sqrt(size)
    for n in range(1, size):
        level = n.bit_length() - 1
        k = n - (1 << level)
        support = size >> level
        value = 1.0 / math.sqrt(support)
        matrix[n, k * support : k * support + support // 2] = value
        matrix[n, k * support + support // 2 : (k + 1) * support] = -value
    high = matrix.astype(BF16)
    low = (matrix - high.astype(np.float32)).astype(BF16)
    return high, low


def split3(x):
    hi = x.astype(BF16)
    rest = x - hi.astype(F32)
    mid = rest.astype(BF16)
    low = (rest - mid.astype(F32)).astype(BF16)
    return hi, mid, low


def nn(a, b):
    return lax.dot_general(a, b, (((1,), (0,)), ((), ())), preferred_element_type=F32)


def nt(a, b):
    return lax.dot_general(a, b, (((1,), (1,)), ((), ())), preferred_element_type=F32)


def select_dot(sel, x):
    hi, mid, low = split3(x)
    return nn(sel, hi) + (nn(sel, mid) + nn(sel, low))


def to_rows(x, width):
    q = width // LANES
    return [
        jnp.concatenate([x[i * q + j : i * q + j + 1, :] for j in range(q)], axis=1)
        for i in range(x.shape[0] // q)
    ]


def to_lanes(rows):
    q = rows[0].shape[1] // LANES
    return jnp.concatenate(
        [row[:, j * LANES : (j + 1) * LANES] for row in rows for j in range(q)], axis=0
    )


def total(rows):
    acc = rows[0]
    for row in rows[1:]:
        acc = acc + row
    return jnp.sum(acc, axis=1, keepdims=True)


def kernel(
    n_rows, n_cols, slots,
    rows_hbm, cols_hbm, kept_hbm, depth_hbm, density_hbm,
    tiles_hbm, high_hbm, low_hbm, misfit_hbm, weight_hbm,
    density_out, misfit_out,
    rows_s, cols_s, kept_s, depth_ref, density_ref,
    tiles, high, low, misfit, weight,
    idbuf, colbuf, dotbuf, rowbuf, curvbuf, image_ref, match_ref,
    load_sem, id_send, id_recv, col_send, col_recv, dot_send, dot_recv,
    row_send, row_recv, curv_send, curv_recv,
):
    size = tiles.shape[-1]
    q = size // LANES
    blocks = depth_ref.shape[0] * LANES // size
    mrows = slots * q
    n = n_cols * mrows
    me_r = lax.axis_index("rows")
    me_c = lax.axis_index("cols")

    loads = [
        pltpu.make_async_copy(src, dst, load_sem.at[i])
        for i, (src, dst) in enumerate(
            (
                (kept_hbm, kept_s), (cols_hbm, cols_s), (rows_hbm, rows_s), (depth_hbm, depth_ref),
                (tiles_hbm, tiles), (high_hbm, high), (low_hbm, low),
                (weight_hbm, weight), (misfit_hbm, misfit), (density_hbm, density_ref),
            )
        )
    ]
    for load in loads:
        load.start()

    barrier = pltpu.get_barrier_semaphore()
    for off in range(1, n_cols):
        pl.semaphore_signal(
            barrier, inc=1, device_id={"cols": lax.rem(me_c + off, n_cols)},
            device_id_type=pl.DeviceIdType.MESH,
        )
    for off in range(1, n_rows):
        pl.semaphore_signal(
            barrier, inc=1, device_id={"rows": lax.rem(me_r + off, n_rows)},
            device_id_type=pl.DeviceIdType.MESH,
        )

    def far_first(me, count):
        upper = (2 * me) // count
        for j in range(count - 1):
            down = count - 1 - j
            down = down - lax.select(down <= me, 1, 0)
            up = j + lax.select(j >= me, 1, 0)
            yield down + upper * (up - down)

    def send(buf, axis, me, count, send_sem, recv_sem):
        for peer in far_first(me, count):
            pltpu.make_async_remote_copy(
                src_ref=buf.at[me],
                dst_ref=buf.at[me],
                send_sem=send_sem,
                recv_sem=recv_sem,
                device_id={axis: peer},
                device_id_type=pl.DeviceIdType.MESH,
            ).start()

    def wait_bytes(buf, count, sem):
        view = buf.at[pl.ds(0, count - 1)]
        pltpu.make_async_copy(view, view, sem).wait()

    for load in loads[:5] + loads[7:9]:
        load.wait()
    sub = lax.broadcasted_iota(jnp.int32, (q, LANES), 0)
    own_weight = jnp.concatenate(
        [weight[pl.ds(rows_s[0, s] * q, q), :] for s in range(slots)], axis=0
    )
    own_squared = own_weight * own_weight
    own_codes = jnp.concatenate([rows_s[0, s] * q + sub for s in range(slots)], axis=0)
    idbuf[me_c, 0:mrows, :] = own_squared
    idbuf[me_c, mrows : 2 * mrows, :] = own_codes.astype(F32)
    own_misfit = jnp.concatenate(
        [misfit[pl.ds(rows_s[0, s] * q, q), :] for s in range(slots)], axis=0
    )

    lane = lax.broadcasted_iota(jnp.int32, (1, size), 1)
    hits = [[cols_s[0, s] == b for b in range(blocks)] for s in range(slots)]
    depth = to_rows(depth_ref[...], size)

    sums = [jnp.zeros((1, size), F32) for _ in range(blocks)]
    for s, row in enumerate(to_rows(own_squared * own_misfit, size)):
        product = jnp.where(lane < kept_s[0, s], nn(row.astype(BF16), tiles[s]), 0.0)
        for b in range(blocks):
            sums[b] = sums[b] + jnp.where(hits[s][b], product, 0.0)
    for b in range(blocks):
        rowbuf[0, me_r, b : b + 1, :] = sums[b]
    pl.semaphore_wait(barrier, n_cols + n_rows - 2)
    send(rowbuf.at[0], "rows", me_r, n_rows, row_send.at[0], row_recv.at[0])
    send(idbuf, "cols", me_c, n_cols, id_send.at[0], id_recv.at[0])
    for load in loads[5:7] + loads[9:]:
        load.wait()
    density = to_rows(density_ref[...], size)

    for s in range(slots):
        live = jnp.where(lane < kept_s[0, s], 1.0, 0.0).astype(BF16)
        masked = tiles[s] * live
        cell_weight = jnp.zeros((1, size), F32)
        for b in range(blocks):
            cell_weight = cell_weight + jnp.where(hits[s][b], depth[b], 0.0)
        tiles[s] = ((nn(masked, high[...]) + nn(masked, low[...])) * cell_weight).astype(BF16)

    def adjoint_blocks(field):
        sums = [jnp.zeros((1, size), F32) for _ in range(blocks)]
        for s, row in enumerate(to_rows(field, size)):
            product = nn(row.astype(BF16), tiles[s])
            for b in range(blocks):
                sums[b] = sums[b] + jnp.where(hits[s][b], product, 0.0)
        return sums

    def forward_parts(cells):
        products = []
        for s in range(slots):
            picked = jnp.zeros((1, size), F32)
            for b in range(blocks):
                picked = picked + jnp.where(hits[s][b], cells[b], 0.0)
            products.append(nt(picked.astype(BF16), tiles[s]))
        return to_lanes(products)

    def put_rows(k, sums):
        for b in range(blocks):
            rowbuf[k, me_r, b : b + 1, :] = sums[b]

    def get_rows(k):
        sums = []
        for b in range(blocks):
            acc = rowbuf[k, 0, b : b + 1, :]
            for r in range(1, n_rows):
                acc = acc + rowbuf[k, r, b : b + 1, :]
            sums.append(acc)
        return sums

    wait_bytes(rowbuf.at[0], n_rows, row_recv.at[0])
    terms = [split3(row) for row in get_rows(0)]
    lhs = jnp.concatenate([t[i].astype(F32) for i in range(3) for t in terms], axis=0).astype(BF16)
    back = nn(lhs, high[...]) + nn(lhs, low[...])
    adj = []
    for b in range(blocks):
        at = [back[i * blocks + b : i * blocks + b + 1] for i in range(3)]
        adj.append(depth[b] * (at[0] + (at[1] + at[2])))
    residual = [adj[b] - DAMPING * density[b] for b in range(blocks)]
    direction = None
    solved = None
    norm_prev = dd = None
    parts_dir = image = change = None
    squared = codes = None

    for k in range(ITERS):
        dots = [total([residual[b] * residual[b] for b in range(blocks)])]
        if k:
            dots.append(total([residual[b] * direction[b] for b in range(blocks)]))
        else:
            dots.append(jnp.zeros((1, 1), F32))
        colbuf[k, me_c, :, :] = forward_parts(residual).astype(BF16)
        for i in range(2):
            dotbuf[k, me_c, i : i + 1, :] = jnp.broadcast_to(dots[i], (1, LANES))
        send(colbuf.at[k], "cols", me_c, n_cols, col_send.at[k], col_recv.at[k])
        send(dotbuf.at[k], "cols", me_c, n_cols, dot_send.at[k], dot_recv.at[k])
        if k == 0:
            wait_bytes(idbuf, n_cols, id_recv.at[0])
            codes = idbuf[:, mrows : 2 * mrows, :].reshape(n, LANES)
            squared = idbuf[:, 0:mrows, :].reshape(n, LANES)
            codes_row = jnp.transpose(codes)[0:1, :]
            match_ref[...] = (codes[:, 0:1] == codes_row).astype(F32).astype(BF16)
        wait_bytes(dotbuf.at[k], n_cols, dot_recv.at[k])
        norm = dotbuf[k, 0, 0:1, :]
        cross = dotbuf[k, 0, 1:2, :]
        for c in range(1, n_cols):
            norm = norm + dotbuf[k, c, 0:1, :]
            cross = cross + dotbuf[k, c, 1:2, :]
        wait_bytes(colbuf.at[k], n_cols, col_recv.at[k])
        parts = colbuf[k].reshape(n, LANES)
        new_image = nn(match_ref[...], parts)
        parts = parts.astype(F32)
        if k == 0:
            parts_dir, image = parts, new_image
            direction = residual
            dd = norm
        else:
            beta = norm / norm_prev
            beta_row = jnp.concatenate([beta] * q, axis=1)
            parts_dir = parts + beta * parts_dir
            image = new_image + beta * image
            direction = [residual[b] + beta_row * direction[b] for b in range(blocks)]
            dd = norm + 2.0 * beta * cross + beta * beta * dd
        norm_prev = norm
        curv_part = jnp.sum(
            jnp.sum(parts_dir * (squared * image), axis=0, keepdims=True), axis=1, keepdims=True
        )
        if k + 1 < ITERS:
            image_ref[...] = image
            own_image = image_ref[pl.ds(pl.multiple_of(me_c * mrows, mrows), mrows), :]
            put_rows(k + 1, adjoint_blocks(own_squared * own_image))
            send(rowbuf.at[k + 1], "rows", me_r, n_rows, row_send.at[k + 1], row_recv.at[k + 1])
        curvbuf[k, me_r, :, :] = jnp.broadcast_to(curv_part, (1, LANES))
        send(curvbuf.at[k], "rows", me_r, n_rows, curv_send.at[k], curv_recv.at[k])
        if k + 1 == ITERS:
            share = misfit_out.shape[0]
            wanted = (lax.broadcasted_iota(jnp.int32, (share, n), 0) + me_c * share).astype(F32)
            pick = (wanted == jnp.transpose(codes)[0:1, :]).astype(F32).astype(BF16)
            own_share = misfit[pl.ds(pl.multiple_of(me_c * share, 8), share), :]
            own_share = own_share - select_dot(pick, change)
            last_share = select_dot(pick, parts_dir)
        if k + 1 < ITERS:
            wait_bytes(rowbuf.at[k + 1], n_rows, row_recv.at[k + 1])
            adj = get_rows(k + 1)
        wait_bytes(curvbuf.at[k], n_rows, curv_recv.at[k])
        curv = curvbuf[k, 0, 0:1, :]
        for r in range(1, n_rows):
            curv = curv + curvbuf[k, r, 0:1, :]
        alpha = norm / (curv + DAMPING * dd)
        alpha_row = jnp.concatenate([alpha] * q, axis=1)
        if k == 0:
            solved = [alpha_row * direction[b] for b in range(blocks)]
            change = alpha * parts_dir
        else:
            solved = [solved[b] + alpha_row * direction[b] for b in range(blocks)]
            if k + 1 < ITERS:
                change = change + alpha * parts_dir
        if k + 1 < ITERS:
            residual = [
                residual[b] - alpha_row * (adj[b] + DAMPING * direction[b]) for b in range(blocks)
            ]

    density_out[...] = to_lanes([density[b] + depth[b] * solved[b] for b in range(blocks)])
    misfit_out[...] = own_share - alpha * last_share

    wait_bytes(idbuf, n_cols, id_send.at[0])
    for k in range(ITERS):
        wait_bytes(colbuf.at[k], n_cols, col_send.at[k])
        wait_bytes(dotbuf.at[k], n_cols, dot_send.at[k])
        wait_bytes(rowbuf.at[k], n_rows, row_send.at[k])
        wait_bytes(curvbuf.at[k], n_rows, curv_send.at[k])


def per_device(
    n_rows, n_cols,
    sensitivity, tile_rows, tile_cols, kept_counts, misfit, data_weight, depth_weight, density
):
    slots, size = sensitivity.shape[1], sensitivity.shape[-1]
    q = size // LANES
    data_lanes = misfit.shape[0] // LANES
    cell_lanes = density.shape[0] // LANES
    blocks = density.shape[0] // size
    share = data_lanes // n_cols
    mrows = slots * q
    n = n_cols * mrows
    high, low = haar_matrix(size)
    vmem = pl.BlockSpec(memory_space=pltpu.VMEM)
    hbm = pl.BlockSpec(memory_space=pltpu.HBM)
    dma = pltpu.SemaphoreType.DMA
    new_density, new_misfit = pl.pallas_call(
        functools.partial(kernel, n_rows, n_cols, slots),
        out_shape=(
            jax.ShapeDtypeStruct((cell_lanes, LANES), F32),
            jax.ShapeDtypeStruct((share, LANES), F32),
        ),
        in_specs=[hbm] * 10,
        out_specs=(vmem, vmem),
        scratch_shapes=[
            pltpu.SMEM((1, slots), jnp.int32),
            pltpu.SMEM((1, slots), jnp.int32),
            pltpu.SMEM((1, slots), jnp.int32),
            pltpu.VMEM((cell_lanes, LANES), F32),
            pltpu.VMEM((cell_lanes, LANES), F32),
            pltpu.VMEM((slots, size, size), BF16),
            pltpu.VMEM((size, size), BF16),
            pltpu.VMEM((size, size), BF16),
            pltpu.VMEM((data_lanes, LANES), F32),
            pltpu.VMEM((data_lanes, LANES), F32),
            pltpu.VMEM((n_cols, 2 * mrows, LANES), F32),
            pltpu.VMEM((ITERS, n_cols, mrows, LANES), BF16),
            pltpu.VMEM((ITERS, n_cols, 2, LANES), F32),
            pltpu.VMEM((ITERS, n_rows, blocks, size), F32),
            pltpu.VMEM((ITERS, n_rows, 1, LANES), F32),
            pltpu.VMEM((n, LANES), F32),
            pltpu.VMEM((n, n), BF16),
            dma((10,)), dma((1,)), dma((1,)), dma((ITERS,)), dma((ITERS,)),
            dma((ITERS,)), dma((ITERS,)), dma((ITERS,)), dma((ITERS,)), dma((ITERS,)), dma((ITERS,)),
        ],
        compiler_params=pltpu.CompilerParams(
            collective_id=0, has_side_effects=True, vmem_limit_bytes=67_043_328
        ),
    )(
        tile_rows, tile_cols, kept_counts,
        depth_weight.reshape(cell_lanes, LANES), density.reshape(cell_lanes, LANES),
        sensitivity[0], jnp.asarray(high), jnp.asarray(low),
        misfit.reshape(data_lanes, LANES), data_weight.reshape(data_lanes, LANES),
    )
    return new_density.reshape(-1), new_misfit.reshape(-1)


def solution(mesh):
    return jax.shard_map(
        functools.partial(per_device, mesh.shape["rows"], mesh.shape["cols"]),
        mesh=mesh,
        in_specs=(
            P("rows", "cols", None, None),
            P("rows", "cols"),
            P("rows", "cols"),
            P("rows", "cols"),
            P("rows"),
            P("rows"),
            P("cols"),
            P("cols"),
        ),
        out_specs=(P("cols"), P(("rows", "cols"))),
        check_vma=False,
    )
```

```python
import functools
import math

import jax
import jax.numpy as jnp
import numpy as np
from jax import lax
from jax.experimental import pallas as pl
from jax.experimental.pallas import tpu as pltpu
from jax.sharding import PartitionSpec as P

ITERS = 4
DAMPING = 1.0
LANES = 128
F32 = jnp.float32
BF16 = jnp.bfloat16


def haar_matrix(size):
    matrix = np.zeros((size, size), np.float32)
    matrix[0] = 1.0 / math.sqrt(size)
    for n in range(1, size):
        level = n.bit_length() - 1
        k = n - (1 << level)
        support = size >> level
        value = 1.0 / math.sqrt(support)
        matrix[n, k * support : k * support + support // 2] = value
        matrix[n, k * support + support // 2 : (k + 1) * support] = -value
    high = matrix.astype(BF16)
    low = (matrix - high.astype(np.float32)).astype(BF16)
    return high, low


def split3(x):
    hi = x.astype(BF16)
    rest = x - hi.astype(F32)
    mid = rest.astype(BF16)
    low = (rest - mid.astype(F32)).astype(BF16)
    return hi, mid, low


def nn(a, b):
    return lax.dot_general(a, b, (((1,), (0,)), ((), ())), preferred_element_type=F32)


def nt(a, b):
    return lax.dot_general(a, b, (((1,), (1,)), ((), ())), preferred_element_type=F32)


def select_dot(sel, x):
    hi, mid, low = split3(x)
    return nn(sel, hi) + (nn(sel, mid) + nn(sel, low))


def to_rows(x, width):
    q = width // LANES
    return [
        jnp.concatenate([x[i * q + j : i * q + j + 1, :] for j in range(q)], axis=1)
        for i in range(x.shape[0] // q)
    ]


def to_lanes(rows):
    q = rows[0].shape[1] // LANES
    return jnp.concatenate(
        [row[:, j * LANES : (j + 1) * LANES] for row in rows for j in range(q)], axis=0
    )


def total(rows):
    acc = rows[0]
    for row in rows[1:]:
        acc = acc + row
    return jnp.sum(acc, axis=1, keepdims=True)


def kernel(
    n_rows, n_cols, slots,
    rows_hbm, cols_hbm, kept_hbm, depth_hbm, density_hbm,
    tiles_hbm, high_hbm, low_hbm, misfit_hbm, weight_hbm,
    density_out, misfit_out,
    rows_s, cols_s, kept_s, depth_ref, density_ref,
    tiles, high, low, misfit, weight,
    idbuf, colbuf, dotbuf, rowbuf, curvbuf, image_ref, match_ref,
    load_sem, id_send, id_recv, col_send, col_recv, dot_send, dot_recv,
    row_send, row_recv, curv_send, curv_recv,
):
    size = tiles.shape[-1]
    q = size // LANES
    blocks = depth_ref.shape[0] * LANES // size
    mrows = slots * q
    n = n_cols * mrows
    me_r = lax.axis_index("rows")
    me_c = lax.axis_index("cols")

    loads = [
        pltpu.make_async_copy(src, dst, load_sem.at[i])
        for i, (src, dst) in enumerate(
            (
                (kept_hbm, kept_s), (cols_hbm, cols_s), (rows_hbm, rows_s), (depth_hbm, depth_ref),
                (tiles_hbm, tiles), (high_hbm, high), (low_hbm, low),
                (weight_hbm, weight), (misfit_hbm, misfit), (density_hbm, density_ref),
            )
        )
    ]
    for load in loads:
        load.start()

    barrier = pltpu.get_barrier_semaphore()
    for off in range(1, n_cols):
        pl.semaphore_signal(
            barrier, inc=1, device_id={"cols": lax.rem(me_c + off, n_cols)},
            device_id_type=pl.DeviceIdType.MESH,
        )
    for off in range(1, n_rows):
        pl.semaphore_signal(
            barrier, inc=1, device_id={"rows": lax.rem(me_r + off, n_rows)},
            device_id_type=pl.DeviceIdType.MESH,
        )

    def far_first(me, count):
        upper = (2 * me) // count
        for j in range(count - 1):
            down = count - 1 - j
            down = down - lax.select(down <= me, 1, 0)
            up = j + lax.select(j >= me, 1, 0)
            yield down + upper * (up - down)

    def send(buf, axis, me, count, send_sem, recv_sem):
        for peer in far_first(me, count):
            pltpu.make_async_remote_copy(
                src_ref=buf.at[me],
                dst_ref=buf.at[me],
                send_sem=send_sem,
                recv_sem=recv_sem,
                device_id={axis: peer},
                device_id_type=pl.DeviceIdType.MESH,
            ).start()

    def wait_bytes(buf, count, sem):
        view = buf.at[pl.ds(0, count - 1)]
        pltpu.make_async_copy(view, view, sem).wait()

    for load in loads[:5] + loads[7:9]:
        load.wait()
    sub = lax.broadcasted_iota(jnp.int32, (q, LANES), 0)
    own_weight = jnp.concatenate(
        [weight[pl.ds(rows_s[0, s] * q, q), :] for s in range(slots)], axis=0
    )
    own_squared = own_weight * own_weight
    own_codes = jnp.concatenate([rows_s[0, s] * q + sub for s in range(slots)], axis=0)
    idbuf[me_c, 0:mrows, :] = own_squared
    idbuf[me_c, mrows : 2 * mrows, :] = own_codes.astype(F32)
    own_misfit = jnp.concatenate(
        [misfit[pl.ds(rows_s[0, s] * q, q), :] for s in range(slots)], axis=0
    )

    lane = lax.broadcasted_iota(jnp.int32, (1, size), 1)
    hits = [[cols_s[0, s] == b for b in range(blocks)] for s in range(slots)]
    depth = to_rows(depth_ref[...], size)

    sums = [jnp.zeros((1, size), F32) for _ in range(blocks)]
    for s, row in enumerate(to_rows(own_squared * own_misfit, size)):
        product = jnp.where(lane < kept_s[0, s], nn(row.astype(BF16), tiles[s]), 0.0)
        for b in range(blocks):
            sums[b] = sums[b] + jnp.where(hits[s][b], product, 0.0)
    for b in range(blocks):
        rowbuf[0, me_r, b : b + 1, :] = sums[b]
    pl.semaphore_wait(barrier, n_cols + n_rows - 2)
    send(rowbuf.at[0], "rows", me_r, n_rows, row_send.at[0], row_recv.at[0])
    send(idbuf, "cols", me_c, n_cols, id_send.at[0], id_recv.at[0])
    for load in loads[5:7] + loads[9:]:
        load.wait()
    density = to_rows(density_ref[...], size)

    for s in range(slots):
        live = jnp.where(lane < kept_s[0, s], 1.0, 0.0).astype(BF16)
        masked = tiles[s] * live
        cell_weight = jnp.zeros((1, size), F32)
        for b in range(blocks):
            cell_weight = cell_weight + jnp.where(hits[s][b], depth[b], 0.0)
        tiles[s] = ((nn(masked, high[...]) + nn(masked, low[...])) * cell_weight).astype(BF16)

    def adjoint_blocks(field):
        sums = [jnp.zeros((1, size), F32) for _ in range(blocks)]
        for s, row in enumerate(to_rows(field, size)):
            product = nn(row.astype(BF16), tiles[s])
            for b in range(blocks):
                sums[b] = sums[b] + jnp.where(hits[s][b], product, 0.0)
        return sums

    def forward_parts(cells):
        products = []
        for s in range(slots):
            picked = jnp.zeros((1, size), F32)
            for b in range(blocks):
                picked = picked + jnp.where(hits[s][b], cells[b], 0.0)
            products.append(nt(picked.astype(BF16), tiles[s]))
        return to_lanes(products)

    def put_rows(k, sums):
        for b in range(blocks):
            rowbuf[k, me_r, b : b + 1, :] = sums[b]

    def get_rows(k):
        sums = []
        for b in range(blocks):
            acc = rowbuf[k, 0, b : b + 1, :]
            for r in range(1, n_rows):
                acc = acc + rowbuf[k, r, b : b + 1, :]
            sums.append(acc)
        return sums

    wait_bytes(rowbuf.at[0], n_rows, row_recv.at[0])
    terms = [split3(row) for row in get_rows(0)]
    lhs = jnp.concatenate([t[i].astype(F32) for i in range(3) for t in terms], axis=0).astype(BF16)
    back = nn(lhs, high[...]) + nn(lhs, low[...])
    adj = []
    for b in range(blocks):
        at = [back[i * blocks + b : i * blocks + b + 1] for i in range(3)]
        adj.append(depth[b] * (at[0] + (at[1] + at[2])))
    residual = [adj[b] - DAMPING * density[b] for b in range(blocks)]
    direction = None
    solved = None
    norm_prev = dd = None
    parts_dir = image = change = None
    squared = codes = None

    for k in range(ITERS):
        dots = [total([residual[b] * residual[b] for b in range(blocks)])]
        if k:
            dots.append(total([residual[b] * direction[b] for b in range(blocks)]))
        else:
            dots.append(jnp.zeros((1, 1), F32))
        colbuf[k, me_c, :, :] = forward_parts(residual).astype(BF16)
        for i in range(2):
            dotbuf[k, me_c, i : i + 1, :] = jnp.broadcast_to(dots[i], (1, LANES))
        send(colbuf.at[k], "cols", me_c, n_cols, col_send.at[0], col_recv.at[k])
        send(dotbuf.at[k], "cols", me_c, n_cols, dot_send.at[0], dot_recv.at[k])
        if k == 0:
            wait_bytes(idbuf, n_cols, id_recv.at[0])
            codes = idbuf[:, mrows : 2 * mrows, :].reshape(n, LANES)
            squared = idbuf[:, 0:mrows, :].reshape(n, LANES)
            codes_row = jnp.transpose(codes)[0:1, :]
            match_ref[...] = (codes[:, 0:1] == codes_row).astype(F32).astype(BF16)
        wait_bytes(dotbuf.at[k], n_cols, dot_recv.at[k])
        norm = dotbuf[k, 0, 0:1, :]
        cross = dotbuf[k, 0, 1:2, :]
        for c in range(1, n_cols):
            norm = norm + dotbuf[k, c, 0:1, :]
            cross = cross + dotbuf[k, c, 1:2, :]
        wait_bytes(colbuf.at[k], n_cols, col_recv.at[k])
        parts = colbuf[k].reshape(n, LANES)
        new_image = nn(match_ref[...], parts)
        parts = parts.astype(F32)
        if k == 0:
            parts_dir, image = parts, new_image
            direction = residual
            dd = norm
        else:
            beta = norm / norm_prev
            beta_row = jnp.concatenate([beta] * q, axis=1)
            parts_dir = parts + beta * parts_dir
            image = new_image + beta * image
            direction = [residual[b] + beta_row * direction[b] for b in range(blocks)]
            dd = norm + 2.0 * beta * cross + beta * beta * dd
        norm_prev = norm
        curv_part = jnp.sum(
            jnp.sum(parts_dir * (squared * image), axis=0, keepdims=True), axis=1, keepdims=True
        )
        if k + 1 < ITERS:
            image_ref[...] = image
            own_image = image_ref[pl.ds(pl.multiple_of(me_c * mrows, mrows), mrows), :]
            put_rows(k + 1, adjoint_blocks(own_squared * own_image))
            send(rowbuf.at[k + 1], "rows", me_r, n_rows, row_send.at[0], row_recv.at[k + 1])
        curvbuf[k, me_r, :, :] = jnp.broadcast_to(curv_part, (1, LANES))
        send(curvbuf.at[k], "rows", me_r, n_rows, curv_send.at[0], curv_recv.at[k])
        if k + 1 == ITERS:
            share = misfit_out.shape[0]
            wanted = (lax.broadcasted_iota(jnp.int32, (share, n), 0) + me_c * share).astype(F32)
            pick = (wanted == jnp.transpose(codes)[0:1, :]).astype(F32).astype(BF16)
            own_share = misfit[pl.ds(pl.multiple_of(me_c * share, 8), share), :]
            own_share = own_share - select_dot(pick, change)
            last_share = select_dot(pick, parts_dir)
        if k + 1 < ITERS:
            wait_bytes(rowbuf.at[k + 1], n_rows, row_recv.at[k + 1])
            adj = get_rows(k + 1)
        wait_bytes(curvbuf.at[k], n_rows, curv_recv.at[k])
        curv = curvbuf[k, 0, 0:1, :]
        for r in range(1, n_rows):
            curv = curv + curvbuf[k, r, 0:1, :]
        alpha = norm / (curv + DAMPING * dd)
        alpha_row = jnp.concatenate([alpha] * q, axis=1)
        if k == 0:
            solved = [alpha_row * direction[b] for b in range(blocks)]
            change = alpha * parts_dir
        else:
            solved = [solved[b] + alpha_row * direction[b] for b in range(blocks)]
            if k + 1 < ITERS:
                change = change + alpha * parts_dir
        if k + 1 < ITERS:
            residual = [
                residual[b] - alpha_row * (adj[b] + DAMPING * direction[b]) for b in range(blocks)
            ]

    density_out[...] = to_lanes([density[b] + depth[b] * solved[b] for b in range(blocks)])
    misfit_out[...] = own_share - alpha * last_share

    wait_bytes(idbuf, n_cols, id_send.at[0])
    for buf, count, sem in (
        (colbuf, n_cols, col_send), (dotbuf, n_cols, dot_send),
        (rowbuf, n_rows, row_send), (curvbuf, n_rows, curv_send),
    ):
        view = buf.at[:, pl.ds(0, count - 1)]
        pltpu.make_async_copy(view, view, sem.at[0]).wait()


def per_device(
    n_rows, n_cols,
    sensitivity, tile_rows, tile_cols, kept_counts, misfit, data_weight, depth_weight, density
):
    slots, size = sensitivity.shape[1], sensitivity.shape[-1]
    q = size // LANES
    data_lanes = misfit.shape[0] // LANES
    cell_lanes = density.shape[0] // LANES
    blocks = density.shape[0] // size
    share = data_lanes // n_cols
    mrows = slots * q
    n = n_cols * mrows
    high, low = haar_matrix(size)
    vmem = pl.BlockSpec(memory_space=pltpu.VMEM)
    hbm = pl.BlockSpec(memory_space=pltpu.HBM)
    dma = pltpu.SemaphoreType.DMA
    new_density, new_misfit = pl.pallas_call(
        functools.partial(kernel, n_rows, n_cols, slots),
        out_shape=(
            jax.ShapeDtypeStruct((cell_lanes, LANES), F32),
            jax.ShapeDtypeStruct((share, LANES), F32),
        ),
        in_specs=[hbm] * 10,
        out_specs=(vmem, vmem),
        scratch_shapes=[
            pltpu.SMEM((1, slots), jnp.int32),
            pltpu.SMEM((1, slots), jnp.int32),
            pltpu.SMEM((1, slots), jnp.int32),
            pltpu.VMEM((cell_lanes, LANES), F32),
            pltpu.VMEM((cell_lanes, LANES), F32),
            pltpu.VMEM((slots, size, size), BF16),
            pltpu.VMEM((size, size), BF16),
            pltpu.VMEM((size, size), BF16),
            pltpu.VMEM((data_lanes, LANES), F32),
            pltpu.VMEM((data_lanes, LANES), F32),
            pltpu.VMEM((n_cols, 2 * mrows, LANES), F32),
            pltpu.VMEM((ITERS, n_cols, mrows, LANES), BF16),
            pltpu.VMEM((ITERS, n_cols, 2, LANES), F32),
            pltpu.VMEM((ITERS, n_rows, blocks, size), F32),
            pltpu.VMEM((ITERS, n_rows, 1, LANES), F32),
            pltpu.VMEM((n, LANES), F32),
            pltpu.VMEM((n, n), BF16),
            dma((10,)), dma((1,)), dma((1,)), dma((1,)), dma((ITERS,)),
            dma((1,)), dma((ITERS,)), dma((1,)), dma((ITERS,)), dma((1,)), dma((ITERS,)),
        ],
        compiler_params=pltpu.CompilerParams(
            collective_id=0, has_side_effects=True, vmem_limit_bytes=67_043_328
        ),
    )(
        tile_rows, tile_cols, kept_counts,
        depth_weight.reshape(cell_lanes, LANES), density.reshape(cell_lanes, LANES),
        sensitivity[0], jnp.asarray(high), jnp.asarray(low),
        misfit.reshape(data_lanes, LANES), data_weight.reshape(data_lanes, LANES),
    )
    return new_density.reshape(-1), new_misfit.reshape(-1)


def solution(mesh):
    return jax.shard_map(
        functools.partial(per_device, mesh.shape["rows"], mesh.shape["cols"]),
        mesh=mesh,
        in_specs=(
            P("rows", "cols", None, None),
            P("rows", "cols"),
            P("rows", "cols"),
            P("rows", "cols"),
            P("rows"),
            P("rows"),
            P("cols"),
            P("cols"),
        ),
        out_specs=(P("cols"), P(("rows", "cols"))),
        check_vma=False,
    )
```
